128 devices in a mesh: brow: 8 (over x_hi, y), bcol: 16 (over z, x_lo, core).
Axes of the slice: x: 4 (x_hi: 2, x_lo: 2; x = x_hi * 2 + x_lo), y: 4, z: 4, core: 2. Of those that a mesh axis runs over, the one named last changes fastest.
Arguments:
- panel_points: bfloat16 [3, 24576], P(None, ('brow', 'bcol')), may hold values from 0 to 1
- panel_map: int32 [3, 24576], replicated, may hold values from 0 to 2047, as said below
- element_nodes: int32 [125, 4096], P(None, ('brow', 'bcol')), may hold values from 0 to 2047
- element_coef: float32 [4096], P(('brow', 'bcol')), may hold values from 0.1 to 1
- element_matrix: float32 [125, 125], replicated, as said below
- node_mass: float32 [262144], P(('brow', 'bcol')), may hold values from 2 to 4
- forcing: float32 [64, 262144], P(None, ('brow', 'bcol')), may hold values from -6 to 6
- field_start: float32 [64, 262144], P(None, ('brow', 'bcol')), may hold values from -6 to 6
- potential_start: float32 [64, 24576], P(None, ('brow', 'bcol')), may hold values from -6 to 6
Outputs:
- fem_field: float32 [64, 262144], P(None, ('brow', 'bcol'))
- potential: float32 [64, 24576], P(None, ('brow', 'bcol'))
The draws below stay inside these ranges and needn't reach their ends.
Inputs may be any that keep to these rules, and one draw needn't show every extreme that they name: `panel_map`: row 0 is an index over brow+bcol (brow slowest), row 2 a local node below 2048. In each aligned block of 192 panels every group owns either no panel or exactly 3 of them, whose row 1 values are 0 to 2, each once. `element_nodes`: local node numbers within the element's own group. `element_matrix`: Symmetric.
All inputs are finite; a program needn't handle non-finite values.
Results may differ from the reference program's by a relative error of at most 0.0015.
The reference program's roundings to bfloat16 on the way (of `densities`, `loads` and `turned`) count: a program that leaves them out, or rounds other values in their place, can miss the bound.
Values may be sent and summed in bfloat16 or wider, within the bound.
A program may use at most 128 MiB of HBM per device.

```python
import math
import jax
import jax.numpy as jnp
from jax import lax

RHS = 32
COLS = 64
PANEL_DEV = 192
PANELS = 24576
CAP = 3
NPE = 125
ELEM_DEV = 32
ELEMENTS = 4096
NODES_DEV = 2048
NODES = 262144
RIM = 128
SWEEPS = 3
ITERS = 2
DEVICES = 128


def draw_panel_map(key, part):
    blocks = PANELS // PANEL_DEV
    owners = PANEL_DEV // CAP
    key_bias, key_noise, key_order, key_node = jax.random.split(jax.random.fold_in(key, 11), 4)
    owner_bias = jax.random.permutation(key_bias, blocks).astype(jnp.int32)
    random_part = jax.random.randint(key_noise, (blocks, blocks), 0, blocks, dtype=jnp.int32)
    scores = (random_part + owner_bias[None, :]) * blocks + jnp.arange(blocks, dtype=jnp.int32)[None, :]
    values_top, chosen = lax.top_k(scores, owners)
    positions = jnp.arange(PANEL_DEV, dtype=jnp.int32)
    owner_seq = jnp.take(chosen.astype(jnp.int32), positions // CAP, axis=1)
    slot_seq = jnp.broadcast_to(positions % CAP, (blocks, PANEL_DEV))
    sort_keys = jax.random.randint(key_order, (blocks, PANEL_DEV), 0, PANEL_DEV, dtype=jnp.int32) * PANEL_DEV + positions[None, :]
    ordering = jnp.argsort(sort_keys, axis=1, stable=True)
    panel_owner = jnp.take_along_axis(owner_seq, ordering, axis=1).reshape(-1)
    panel_slot = jnp.take_along_axis(slot_seq, ordering, axis=1).reshape(-1)
    local_node = jax.random.randint(key_node, (PANELS,), 0, NODES_DEV, dtype=jnp.int32)
    return jnp.stack([panel_owner, panel_slot, local_node]).astype(jnp.int32)


def draw_element_matrix(key, part):
    key_off, key_diag = jax.random.split(jax.random.fold_in(key, 23))
    entries = jax.random.normal(key_off, (NPE, NPE), jnp.float32)
    coupling_part = (entries + entries.T) * (0.5 / math.sqrt(2.0 * NPE))
    diagonal_part = jax.random.uniform(key_diag, (NPE,), jnp.float32, 1.0, 2.0)
    return (coupling_part + jnp.diag(diagonal_part)).astype(jnp.float32)


def plant(values, stream_key, least, high):
    place = [jax.random.randint(jax.random.fold_in(stream_key, axis), (), 0, length) for axis, length in enumerate(values.shape)]
    main_axis = values.shape.index(max(values.shape))
    beside = place[:main_axis] + [(place[main_axis] + 1) % values.shape[main_axis]] + place[main_axis + 1:]
    return values.at[tuple(place)].set(least).at[tuple(beside)].set(high)


def level_of(key, extent, cuts, low, top_value):
    level = 1.0
    for position, blocks in cuts:
        heights = jax.random.uniform(jax.random.fold_in(jax.random.fold_in(key, 6), position), (blocks,), jnp.float32, low / len(cuts), top_value / len(cuts))
        level = level * jnp.repeat(jnp.exp(heights), extent[position] // blocks).reshape((-1,) + (1,) * (len(extent) - 1 - position))
    return level


def noise(rng, shape, deviation, bound, shards=(), kind=jnp.bfloat16):
    level = level_of(rng, shape, shards, -0.22, 0.18) if shards else 1.0
    values = jax.random.normal(rng, shape, jnp.float32) * deviation * level
    return jnp.minimum(jnp.maximum(values, -bound), bound).astype(kind)


def setup_inputs(seed: int = 0) -> dict:
    seeds = jax.random.split(jax.random.key(seed), 10)
    return {
        "panel_points": jnp.clip(1.0 * jax.random.uniform(seeds[0], (3, PANELS), jnp.float32) ** level_of(seeds[0], (3, PANELS), ((1, 128),), -0.2, 0.2), 0.0, 1.0).astype(jnp.bfloat16),
        "panel_map": draw_panel_map(jax.random.fold_in(seeds[9], 71), 0),
        "element_nodes": plant(jax.random.randint(seeds[2], (NPE, ELEMENTS), 0, NODES_DEV), jax.random.fold_in(seeds[2], 1), 0, NODES_DEV - 1).astype(jnp.int32),
        "element_coef": jnp.clip(jnp.exp(math.log(1.0) - 2.3025851 * jax.random.uniform(seeds[3], (ELEMENTS,), jnp.float32) ** level_of(seeds[3], (ELEMENTS,), ((0, 128),), -0.2, 0.2)), 0.1, 1.0),
        "element_matrix": draw_element_matrix(jax.random.fold_in(seeds[9], 71), 0),
        "node_mass": jnp.clip(2.0 + 2.0 * jax.random.uniform(seeds[5], (NODES,), jnp.float32) ** level_of(seeds[5], (NODES,), ((0, 128),), -0.2, 0.2), 2.0, 4.0),
        "forcing": noise(seeds[6], (COLS, NODES), 1.0, 6.0, ((1, 128),), jnp.float32),
        "field_start": noise(seeds[7], (COLS, NODES), 1.0, 6.0, ((1, 128),), jnp.float32),
        "potential_start": noise(seeds[8], (COLS, PANELS), 1.0, 6.0, ((1, 128),), jnp.float32),
    }


wave_number = 20.0
penalty = 0.5

def kernel_pair(sources, targets, count_all):
    src_xyz = sources.astype(jnp.float32)
    tgt_xyz = targets.astype(jnp.float32)
    delta_xyz = src_xyz[:, :, None] - tgt_xyz[:, None, :]
    dist_sq = lax.optimization_barrier(jnp.sum(delta_xyz * delta_xyz, axis=0))
    soften = 0.5 * float(count_all) ** (-1.0 / 3.0)
    radius = jnp.sqrt(dist_sq + soften * soften)
    scaling = 1.0 / (radius * math.sqrt(float(count_all)))
    real_tile = (jnp.cos(wave_number * radius) * scaling).astype(jnp.bfloat16)
    imag_tile = (jnp.sin(wave_number * radius) * scaling).astype(jnp.bfloat16)
    return (real_tile, imag_tile)

def bem_apply(densities, panel_points):
    turned = jnp.concatenate([-densities[RHS:], densities[:RHS]], axis=0).astype(jnp.float32)
    dense_full = densities.astype(jnp.float32)
    target_blocks = panel_points.reshape(3, DEVICES, PANEL_DEV).transpose(1, 0, 2)

    def one_block(targets):
        real_tile, imag_tile = kernel_pair(panel_points, targets, PANELS)
        first = jnp.dot(dense_full, real_tile.astype(jnp.float32), precision=lax.Precision.HIGHEST)
        second = jnp.dot(turned, imag_tile.astype(jnp.float32), precision=lax.Precision.HIGHEST)
        return first + second
    result = lax.map(one_block, target_blocks)
    return result.transpose(1, 0, 2).reshape(COLS, PANELS)

def operate(field_now, global_nodes, element_coef, element_matrix, node_mass):
    gathered = jnp.take(field_now, global_nodes, axis=1)
    stiffness = jnp.einsum('jk,cke->cje', element_matrix, gathered, precision=lax.Precision.HIGHEST) * element_coef
    result = node_mass * field_now + jnp.zeros_like(field_now).at[:, global_nodes].add(stiffness)
    shaped = field_now.reshape(COLS, DEVICES, NODES_DEV)
    zero_rim = jnp.zeros((COLS, 1, RIM), jnp.float32)
    from_left = jnp.concatenate([zero_rim, shaped[:, :-1, NODES_DEV - RIM:]], axis=1)
    from_right = jnp.concatenate([shaped[:, 1:, :RIM], zero_rim], axis=1)
    middle = jnp.zeros((COLS, DEVICES, NODES_DEV - 2 * RIM), jnp.float32)
    couple = jnp.concatenate([from_left, middle, from_right], axis=2).reshape(COLS, NODES)
    return result - penalty * couple

def reference(panel_points, panel_map, element_nodes, element_coef, element_matrix, node_mass, forcing, field_start, potential_start):
    panel_node = (panel_map[0] * NODES_DEV + panel_map[2]).astype(jnp.int32)
    group_base = (jnp.arange(ELEMENTS, dtype=jnp.int32) // ELEM_DEV * NODES_DEV).astype(jnp.int32)
    global_nodes = (element_nodes + group_base[None, :]).astype(jnp.int32)
    field_now = field_start
    potential_now = potential_start
    for turn_index in range(ITERS):
        densities = jnp.take(field_now, panel_node, axis=1).astype(jnp.bfloat16)
        loads = lax.optimization_barrier(potential_now.astype(jnp.bfloat16)).astype(jnp.float32)
        rhs = forcing + jnp.zeros_like(forcing).at[:, panel_node].add(loads)
        new_field = field_now
        for sweep in range(SWEEPS):
            weight = 1.0 / (1.25 + 0.75 * math.cos(math.pi * (2 * sweep + 1) / (2.0 * SWEEPS)))
            residual = rhs - operate(new_field, global_nodes, element_coef, element_matrix, node_mass)
            new_field = new_field + weight * residual / node_mass
        potential_now = bem_apply(densities, panel_points)
        field_now = new_field
    return (field_now, potential_now)
```

```python
import functools
import math

import jax
import jax.numpy as jnp
from jax import lax
from jax.experimental import pallas as pl
from jax.experimental.pallas import tpu as pltpu
from jax.sharding import PartitionSpec as P

F32 = jnp.float32
BF16 = jnp.bfloat16
MESH = pl.DeviceIdType.MESH
VMEM = pl.BlockSpec(memory_space=pltpu.VMEM)
ANY = pl.BlockSpec(memory_space=pl.ANY)

RIM = 128
SWEEPS = 3
ITERS = 2
WAVE = 20.0
PENALTY = 0.5
COLS = 64
NODES = 2048
ELEMS = 32
PAD = 128
PANELS = 192
HALF = PANELS // 2
DEVICES = 128
COUNT = PANELS * DEVICES
BCOL = 16
SLAB = 8
CHUNK = 512

WEIGHTS = [
    1.0 / (1.25 + 0.75 * math.cos(math.pi * (2 * m + 1) / (2.0 * SWEEPS))) for m in range(SWEEPS)
]
SOFT2 = (0.5 * float(COUNT) ** (-1.0 / 3.0)) ** 2
NORM = 1.0 / math.sqrt(float(COUNT))
TURN = WAVE / (2.0 * math.pi)
SIN_C = (4.442882919124344, -7.308245686509072, 3.606354218432951, -0.8461116503739222, 0.10982451642504502)
COS_C = (1.4142134962552282, -6.978850948563825, 5.739460376907423, -1.8835579059881276, 0.3106880275291379)


def split(x):
    hi = x.astype(BF16)
    return hi, (x - hi.astype(F32)).astype(BF16)


def dot(a, b):
    return jnp.dot(a, b, preferred_element_type=F32)


def dot_t(a, b):
    return lax.dot_general(a, b, (((1,), (1,)), ((), ())), preferred_element_type=F32)


def dot_l(a, b):
    return lax.dot_general(a, b, (((0,), (0,)), ((), ())), preferred_element_type=F32)


def place(rank):
    return (rank // BCOL, rank % BCOL)


def fem_kernel(
    first,
    refs,
):
    if first:
        (map_ref, own_ref, idx_ref, idxt_ref, mat_ref, coef_ref, mass_ref, force_ref, field_ref, pot_ref, pts_ref,
         out_ref, dens_ref, ptsall_ref,
         gn, gt, v2, yy, rhs, rmass, send, recv, dbuf, rim_out, rim_in, tab,
         a2a_s, a2a_r, ag_s, ag_r, sib_s, sib_r, rim_s, rim_r, loc_s,
         pts_in, pag_s, pag_r, psib_s, psib_r) = refs
    else:
        (map_ref, own_ref, idx_ref, idxt_ref, mat_ref, coef_ref, mass_ref, force_ref, field_ref, pot_ref,
         out_ref, dens_ref,
         gn, gt, v2, yy, rhs, rmass, send, recv, dbuf, rim_out, rim_in, tab,
         a2a_s, a2a_r, ag_s, ag_r, sib_s, sib_r, rim_s, rim_r, loc_s) = refs
    row, col = lax.axis_index("brow"), lax.axis_index("bcol")
    me = row * BCOL + col
    core = col % 2
    chip = me // 2
    sibling = (row, col + 1 - 2 * core)

    barrier = pltpu.get_barrier_semaphore()

    def greet(k, carry):
        pl.semaphore_signal(barrier, inc=1, device_id=place((me + k) % DEVICES), device_id_type=MESH)
        return carry

    lax.fori_loop(1, DEVICES, greet, 0)

    owner, slot, node = map_ref[0], map_ref[1], map_ref[2]
    mine = owner == me
    field16 = field_ref[...].astype(BF16)
    traces, loads = [], []
    own_owner = map_ref[0, pl.ds(me, 1), :]
    own_slot = map_ref[1, pl.ds(me, 1), :]
    pot16 = pot_ref[...].astype(BF16)
    for s in range(3):
        here = jnp.where(mine & (slot == s), node + 1, 0)
        at = jnp.sum(here, axis=1, keepdims=True) - 1
        table = jnp.where(lax.broadcasted_iota(jnp.int32, (DEVICES, NODES), 1) == at, 1.0, 0.0).astype(BF16)
        tab[s * DEVICES:(s + 1) * DEVICES, :] = table
        traces.append(dot_t(table, field16))
        pick = (lax.broadcasted_iota(jnp.int32, (DEVICES, PANELS), 0) == own_owner) & (own_slot == s)
        loads.append(dot_t(jnp.where(pick, 1.0, 0.0).astype(BF16), pot16))
    for r, (a, b) in enumerate(((traces[0], traces[1]), (traces[2], loads[2]), (loads[0], loads[1]))):
        send[pl.ds(r, DEVICES, stride=SLAB), :] = jnp.concatenate([a, b], axis=1)

    pl.semaphore_wait(barrier, DEVICES - 1)

    def slab(ref, k):
        return ref.at[pl.ds(pl.multiple_of(k * SLAB, SLAB), SLAB), :]

    def push(k, carry):
        to = (me + k) % DEVICES
        pltpu.make_async_remote_copy(
            src_ref=slab(send, to), dst_ref=slab(recv, me), send_sem=a2a_s, recv_sem=a2a_r,
            device_id=place(to), device_id_type=MESH,
        ).start()
        return carry

    lax.fori_loop(1, DEVICES, push, 0)

    def rim_copy(sweep, side):
        return pltpu.make_async_remote_copy(
            src_ref=rim_out.at[sweep, side], dst_ref=rim_in.at[sweep, 1 - side], send_sem=rim_s.at[sweep, side],
            recv_sem=rim_r.at[sweep, 1 - side], device_id=place(me + 2 * side - 1), device_id_type=MESH,
        )

    def rim_send(sweep, side):
        @pl.when((me > 0) if side == 0 else (me < DEVICES - 1))
        def _():
            rim_copy(sweep, side).start()

    for side in range(2):
        rim_out[0, side] = field_ref[:, side * (NODES - RIM):side * (NODES - RIM) + RIM]
        rim_send(0, side)

    if first:
        def pts_push(k, carry):
            to = ((chip + k) % (DEVICES // 2)) * 2 + core
            pltpu.make_async_remote_copy(
                src_ref=pts_ref, dst_ref=pts_in.at[core * 64 + chip], send_sem=pag_s, recv_sem=pag_r,
                device_id=place(to), device_id_type=MESH,
            ).start()
            return carry

        lax.fori_loop(1, DEVICES // 2, pts_push, 0)
        pts_in[pl.ds(core * 64 + chip, 1)] = pts_ref[...][None]

    recv[pl.ds(pl.multiple_of(me * SLAB, SLAB), SLAB), :] = send[pl.ds(pl.multiple_of(me * SLAB, SLAB), SLAB), :]

    def table_gt(e, carry):
        at = jnp.sum(
            jnp.where(lax.broadcasted_iota(jnp.int32, (PAD, ELEMS), 1) == e, idx_ref[...] + 1, 0), axis=1, keepdims=True
        ) - 1
        base = pl.multiple_of(e * PAD, PAD)
        for h in range(4):
            lane = lax.broadcasted_iota(jnp.int32, (PAD, 512), 1) + h * 512
            gt[pl.ds(base, PAD), h * 512:(h + 1) * 512] = jnp.where(lane == at, 1.0, 0.0).astype(BF16)
        ids = idxt_ref[pl.ds(e, 1), :]

        def rows(h, inner):
            start = pl.multiple_of(h * 256, 256)
            line = lax.broadcasted_iota(jnp.int32, (256, PAD), 0) + start
            gn[pl.ds(start, 256), pl.ds(base, PAD)] = jnp.where(line == ids, 1.0, 0.0).astype(BF16)
            return inner

        lax.fori_loop(0, NODES // 256, rows, 0, unroll=2)
        return carry

    lax.fori_loop(0, ELEMS, table_gt, 0)
    rmass[...] = 1.0 / mass_ref[...]
    out_ref[...] = field_ref[...]
    hi, lo = split(field_ref[...])
    v2[0:COLS, :] = hi
    v2[COLS:, :] = lo

    whole = pl.ds(0, (DEVICES - 1) * SLAB)
    arrived = pltpu.make_async_remote_copy(
        src_ref=send.at[whole, :], dst_ref=recv.at[whole, :], send_sem=a2a_s, recv_sem=a2a_r,
        device_id=sibling, device_id_type=MESH,
    )
    arrived.wait_recv()
    got = [recv[pl.ds(r, DEVICES, stride=SLAB), :] for r in range(3)]
    got_trace = [got[0][:, :COLS], got[0][:, COLS:], got[1][:, :COLS]]
    got_load = [got[2][:, :COLS], got[2][:, COLS:], got[1][:, COLS:]]
    own = own_ref[...]
    dens = jnp.zeros((PANELS, COLS), F32)
    for s in range(3):
        pick = (lax.broadcasted_iota(jnp.int32, (PANELS, DEVICES), 1) == own[:, 0:1]) & (own[:, 1:2] == s)
        dens += dot(jnp.where(pick, 1.0, 0.0).astype(BF16), got_trace[s].astype(BF16))
    dbuf[...] = jnp.concatenate([dens[:HALF], dens[HALF:]], axis=1).astype(BF16)
    keep = pltpu.make_async_copy(dbuf, dens_ref.at[core * 64 + chip], loc_s)
    keep.start()

    def dens_push(k, carry):
        to = ((chip + k) % (DEVICES // 2)) * 2 + core
        pltpu.make_async_remote_copy(
            src_ref=dbuf, dst_ref=dens_ref.at[core * 64 + chip], send_sem=ag_s, recv_sem=ag_r,
            device_id=place(to), device_id_type=MESH,
        ).start()
        return carry

    lax.fori_loop(1, DEVICES // 2, dens_push, 0)
    load_t = jnp.concatenate(got_load, axis=0).T.astype(BF16)
    for h in range(NODES // CHUNK):
        c = slice(h * CHUNK, (h + 1) * CHUNK)
        rhs[:, c] = force_ref[:, c] + dot(load_t, tab[:, c])

    def forward_dens():
        group = pl.ds(0, 63)
        wait = pltpu.make_async_remote_copy(
            src_ref=dens_ref.at[group], dst_ref=dens_ref.at[group], send_sem=ag_s, recv_sem=ag_r,
            device_id=sibling, device_id_type=MESH,
        )
        wait.wait_recv()
        wait.wait_send()
        keep.wait()
        half = dens_ref.at[pl.ds(core * 64, 64)]
        swap = pltpu.make_async_remote_copy(
            src_ref=half, dst_ref=half, send_sem=sib_s, recv_sem=sib_r, device_id=sibling, device_id_type=MESH,
        )
        swap.start()
        if first:
            wait = pltpu.make_async_remote_copy(
                src_ref=pts_in.at[group], dst_ref=pts_in.at[group], send_sem=pag_s, recv_sem=pag_r,
                device_id=sibling, device_id_type=MESH,
            )
            wait.wait_recv()
            wait.wait_send()
            phalf = pts_in.at[pl.ds(core * 64, 64)]
            pswap = pltpu.make_async_remote_copy(
                src_ref=phalf, dst_ref=phalf, send_sem=psib_s, recv_sem=psib_r, device_id=sibling, device_id_type=MESH,
            )
            pswap.start()
            return swap, pswap
        return (swap,)

    def rim_wait(sweep):
        @pl.when(me > 0)
        def _():
            rim_copy(sweep, 1).wait_recv()
            rim_copy(sweep, 0).wait_send()

        @pl.when(me == 0)
        def _():
            rim_in[sweep, 0] = jnp.zeros((COLS, RIM), F32)

        @pl.when(me < DEVICES - 1)
        def _():
            rim_copy(sweep, 0).wait_recv()
            rim_copy(sweep, 1).wait_send()

        @pl.when(me == DEVICES - 1)
        def _():
            rim_in[sweep, 1] = jnp.zeros((COLS, RIM), F32)

    mat_hi, mat_lo = split(mat_ref[...])
    mat = jnp.concatenate([mat_hi, mat_lo], axis=1)
    for sweep in range(SWEEPS):
        def gather(i, carry):
            c = pl.ds(pl.multiple_of(i * CHUNK, CHUNK), CHUNK)
            got = dot(v2[...], gn[:, c]).astype(BF16)
            per = CHUNK // PAD
            for k in range(per):
                r = dot(got[:, k * PAD:(k + 1) * PAD], mat)
                y = (r[:COLS, :PAD] + (r[:COLS, PAD:] + r[COLS:, :PAD])) * coef_ref[pl.ds(i * per + k, 1), :]
                a, b = split(y)
                e = pl.ds(pl.multiple_of(i * CHUNK + k * PAD, PAD), PAD)
                yy[0:COLS, e] = a
                yy[COLS:, e] = b
            return carry

        lax.fori_loop(0, ELEMS * PAD // CHUNK, gather, 0)
        if sweep == 2:
            swaps = forward_dens()
        rim_wait(sweep)
        last = NODES // CHUNK - 1
        for h in [0, last] + list(range(1, last)):
            c = slice(h * CHUNK, (h + 1) * CHUNK)
            s = dot(yy[...], gt[:, c])
            s = s[:COLS] + s[COLS:]
            if h == 0:
                s = jnp.concatenate([s[:, :RIM] - PENALTY * rim_in[sweep, 0], s[:, RIM:]], axis=1)
            if h == last:
                s = jnp.concatenate([s[:, :CHUNK - RIM], s[:, CHUNK - RIM:] - PENALTY * rim_in[sweep, 1]], axis=1)
            now = out_ref[:, c]
            new = now + WEIGHTS[sweep] * ((rhs[:, c] - s) * rmass[:, c] - now)
            out_ref[:, c] = new
            if sweep < SWEEPS - 1:
                hi, lo = split(new)
                v2[0:COLS, c] = hi
                v2[COLS:, c] = lo
                if h == 0:
                    rim_out[sweep + 1, 0] = new[:, :RIM]
                    rim_send(sweep + 1, 0)
                if h == last:
                    rim_out[sweep + 1, 1] = new[:, CHUNK - RIM:]
                    rim_send(sweep + 1, 1)
    arrived.wait_send()
    for swap in swaps:
        swap.wait()
    if first:
        for g in range(DEVICES // 4):
            four = jnp.concatenate([pts_in[g * 4 + k][:, :HALF] for k in range(4)], axis=1)
            ptsall_ref[:, g * 384:(g + 1) * 384] = four


def fem(first, args):
    out = [
        jax.ShapeDtypeStruct((COLS, NODES), F32),
        jax.ShapeDtypeStruct((DEVICES, HALF, 128), BF16),
    ]
    specs = [VMEM, ANY]
    scratch = [
        pltpu.VMEM((NODES, ELEMS * PAD), BF16),
        pltpu.VMEM((ELEMS * PAD, NODES), BF16),
        pltpu.VMEM((2 * COLS, NODES), BF16),
        pltpu.VMEM((2 * COLS, ELEMS * PAD), BF16),
        pltpu.VMEM((COLS, NODES), F32),
        pltpu.VMEM((1, NODES), F32),
        pltpu.VMEM((DEVICES * SLAB, 128), F32),
        pltpu.VMEM((DEVICES * SLAB, 128), F32),
        pltpu.VMEM((HALF, 128), BF16),
        pltpu.VMEM((SWEEPS, 2, COLS, RIM), F32),
        pltpu.VMEM((SWEEPS, 2, COLS, RIM), F32),
        pltpu.VMEM((3 * DEVICES, NODES), BF16),
    ] + [pltpu.SemaphoreType.DMA] * 6 + [
        pltpu.SemaphoreType.DMA((SWEEPS, 2)),
        pltpu.SemaphoreType.DMA((SWEEPS, 2)),
        pltpu.SemaphoreType.DMA,
    ]
    if first:
        out.append(jax.ShapeDtypeStruct((8, COUNT // 2), F32))
        specs.append(VMEM)
        scratch += [pltpu.VMEM((DEVICES, 8, 128), F32)] + [pltpu.SemaphoreType.DMA] * 4

    def run(*refs):
        fem_kernel(first, refs)

    return pl.pallas_call(
        run,
        out_shape=tuple(out),
        in_specs=[VMEM] * len(args),
        out_specs=tuple(specs),
        scratch_shapes=scratch,
        compiler_params=pltpu.CompilerParams(
            collective_id=1 if first else 2, has_side_effects=True, vmem_limit_bytes=58 << 20
        ),
        name="fem_first" if first else "fem_again",
    )(*args)


def finish(acc, pot_ref):
    real = acc[0:PANELS, :COLS] + acc[2 * PANELS:3 * PANELS, COLS:]
    imag = acc[PANELS:2 * PANELS, :COLS] + acc[3 * PANELS:, COLS:]
    half = COLS // 2
    pot = real + jnp.concatenate([-imag[:, half:], imag[:, :half]], axis=1)
    pot_ref[...] = pot.T


TILE = 256
TILES = COUNT // 2 // TILE
ROWS = 4 * PANELS
STEP = 16


def build_kernel(pts_ref, tgt_ref, dens_ref, store_ref, pot_ref, acc):
    i = pl.program_id(0)

    @pl.when(i == 0)
    def _():
        acc[...] = jnp.zeros_like(acc)

    def rows(r, carry):
        start = pl.multiple_of(r * STEP, STEP)
        for half in range(2):
            for lane in range(TILE // 128):
                c = slice(lane * 128, (lane + 1) * 128)
                d = [
                    pts_ref[half * 3 + k:half * 3 + k + 1, c] - tgt_ref[k, pl.ds(start, STEP), :] for k in range(3)
                ]
                sq = d[0] * d[0] + d[1] * d[1] + (d[2] * d[2] + SOFT2)
                inv = lax.rsqrt(sq)
                turns = (sq * inv) * TURN
                f = turns - jnp.round(turns)
                z = f * f
                sn, cs = SIN_C[4], COS_C[4]
                for k in (3, 2, 1, 0):
                    sn = sn * z + SIN_C[k]
                    cs = cs * z + COS_C[k]
                sn = sn * f
                scale = inv * NORM
                part = sn * scale
                store_ref[0, pl.ds(half * 2 * PANELS + start, STEP), c] = (scale - part * sn).astype(BF16)
                store_ref[0, pl.ds(half * 2 * PANELS + PANELS + start, STEP), c] = (part * cs).astype(BF16)
        return carry

    lax.fori_loop(0, PANELS // STEP, rows, 0, unroll=2)
    acc[...] += dot(store_ref[0], dens_ref[...])

    @pl.when(i == TILES - 1)
    def _():
        finish(acc[...], pot_ref)


def build(pts, tgt, dens):
    return pl.pallas_call(
        build_kernel,
        grid=(TILES,),
        out_shape=(
            jax.ShapeDtypeStruct((TILES, ROWS, TILE), BF16),
            jax.ShapeDtypeStruct((COLS, PANELS), F32),
        ),
        in_specs=[
            pl.BlockSpec((8, TILE), lambda i: (0, i)),
            pl.BlockSpec((3, PANELS, 128), lambda i: (0, 0, 0)),
            pl.BlockSpec((TILE, 128), lambda i: (i, 0)),
        ],
        out_specs=(
            pl.BlockSpec((1, ROWS, TILE), lambda i: (i, 0, 0)),
            pl.BlockSpec((COLS, PANELS), lambda i: (0, 0)),
        ),
        scratch_shapes=[pltpu.VMEM((ROWS, 128), F32)],
        name="bem_build",
    )(pts, tgt, dens)


GROUP = 4


def reuse_kernel(store_ref, dens_ref, pot_ref, acc):
    i = pl.program_id(0)

    @pl.when(i == 0)
    def _():
        acc[...] = jnp.zeros_like(acc)

    for b in range(GROUP):
        acc[...] += dot(store_ref[b], dens_ref[b * TILE:(b + 1) * TILE, :])

    @pl.when(i == TILES // GROUP - 1)
    def _():
        finish(acc[...], pot_ref)


def reuse(store, dens):
    return pl.pallas_call(
        reuse_kernel,
        grid=(TILES // GROUP,),
        out_shape=jax.ShapeDtypeStruct((COLS, PANELS), F32),
        in_specs=[
            pl.BlockSpec((GROUP, ROWS, TILE), lambda i: (i, 0, 0)),
            pl.BlockSpec((GROUP * TILE, 128), lambda i: (i, 0)),
        ],
        out_specs=pl.BlockSpec((COLS, PANELS), lambda i: (0, 0)),
        scratch_shapes=[pltpu.VMEM((ROWS, 128), F32)],
        name="bem_reuse",
    )(store, dens)


def per_device(
    panel_points, panel_map, element_nodes, element_coef, element_matrix, node_mass, forcing, field, potential
):
    me = lax.axis_index("brow") * BCOL + lax.axis_index("bcol")
    npe = element_nodes.shape[0]
    maps = panel_map.reshape(3, DEVICES, PANELS)
    own = lax.dynamic_slice_in_dim(panel_map, me * PANELS, PANELS, axis=1).T
    idx = jnp.pad(element_nodes, ((0, PAD - npe), (0, 0)), constant_values=-1)
    mat = jnp.pad(element_matrix, ((0, PAD - npe), (0, PAD - npe)))
    coef = jnp.broadcast_to(element_coef[:, None], (ELEMS, PAD))
    points = panel_points.astype(F32)
    pts = jnp.pad(
        jnp.concatenate([points[:, :HALF], points[:, HALF:]], axis=0), ((0, 2), (0, 128 - HALF))
    )
    tgt = jnp.broadcast_to(points[:, :, None], (3, PANELS, 128))
    fixed = (maps, own, idx, idx.T, mat, coef, node_mass[None, :], forcing)
    field, dens, pts_all = fem(True, fixed + (field, potential, pts))
    store, potential = build(pts_all, tgt, dens.reshape(COUNT // 2, 128))
    field, dens = fem(False, fixed + (field, potential))
    potential = reuse(store, dens.reshape(COUNT // 2, 128))
    return field, potential


def solution(mesh):
    both = ("brow", "bcol")
    placed = (P(None, both), P(), P(None, both), P(both), P(), P(both), P(None, both), P(None, both), P(None, both))
    return jax.shard_map(
        per_device,
        mesh=mesh,
        in_specs=placed,
        out_specs=(P(None, both), P(None, both)),
        check_vma=False,
    )
```

```python
import functools
import math

import jax
import jax.numpy as jnp
from jax import lax
from jax.experimental import pallas as pl
from jax.experimental.pallas import tpu as pltpu
from jax.sharding import PartitionSpec as P

F32 = jnp.float32
BF16 = jnp.bfloat16
MESH = pl.DeviceIdType.MESH
VMEM = pl.BlockSpec(memory_space=pltpu.VMEM)
ANY = pl.BlockSpec(memory_space=pl.ANY)

RIM = 128
SWEEPS = 3
ITERS = 2
WAVE = 20.0
PENALTY = 0.5
COLS = 64
NODES = 2048
ELEMS = 32
PAD = 128
PANELS = 192
HALF = PANELS // 2
DEVICES = 128
COUNT = PANELS * DEVICES
BCOL = 16
SLAB = 8
CHUNK = 512
STEPS = SWEEPS * ITERS
TILE = 256
GROUP = 3
GROUPS = COUNT // 2 // (TILE * GROUP)
BLOCKS = TILE * GROUP // HALF
ROWS = 4 * PANELS
STEP = 16
UNITS = GROUPS * GROUP * (PANELS // STEP)

WEIGHTS = [
    1.0 / (1.25 + 0.75 * math.cos(math.pi * (2 * m + 1) / (2.0 * SWEEPS))) for m in range(SWEEPS)
]
SOFT2 = (0.5 * float(COUNT) ** (-1.0 / 3.0)) ** 2
NORM = 1.0 / math.sqrt(float(COUNT))
TURN = WAVE / (2.0 * math.pi)
SIN_C = (4.442882919124344, -7.308245686509072, 3.606354218432951, -0.8461116503739222, 0.10982451642504502)
COS_C = (1.4142134962552282, -6.978850948563825, 5.739460376907423, -1.8835579059881276, 0.3106880275291379)


def split(x):
    hi = x.astype(BF16)
    return hi, (x - hi.astype(F32)).astype(BF16)


def dot(a, b):
    return jnp.dot(a, b, preferred_element_type=F32)


def dot_t(a, b):
    return lax.dot_general(a, b, (((1,), (1,)), ((), ())), preferred_element_type=F32)


def dot_l(a, b):
    return lax.dot_general(a, b, (((0,), (0,)), ((), ())), preferred_element_type=F32)


def place(rank):
    return (rank // BCOL, rank % BCOL)


def kernel_tile(d):
    sq = d[0] * d[0] + d[1] * d[1] + (d[2] * d[2] + SOFT2)
    inv = lax.rsqrt(sq)
    turns = (sq * inv) * TURN
    f = turns - jnp.round(turns)
    z = f * f
    sn, cs = SIN_C[4], COS_C[4]
    for k in (3, 2, 1, 0):
        sn = sn * z + SIN_C[k]
        cs = cs * z + COS_C[k]
    sn = sn * f
    scale = inv * NORM
    part = sn * scale
    return (scale - part * sn).astype(BF16), (part * cs).astype(BF16)


def potential_of(acc, first):
    at = first * 128
    real = acc[0:PANELS, at:at + COLS] + acc[2 * PANELS:3 * PANELS, at + COLS:at + 128]
    imag = acc[PANELS:2 * PANELS, at:at + COLS] + acc[3 * PANELS:, at + COLS:at + 128]
    half = COLS // 2
    return (real + jnp.concatenate([-imag[:, half:], imag[:, :half]], axis=1)).T


def body(
    map_ref, idx_ref, mat_ref, mass_ref, force_ref, field_ref, pot_ref, pts_ref, coef_ref,
    out_ref, res_ref, dens0_ref, dens1_ref,
    gn, gt, kmat, v2, yy, rhs, rmass, send, recv, dbuf, rim_out, rim_in, tab, pts_own, pts_in, pts_all, tgt, stream, acc,
    a2a_s, a2a_r, ag_s, ag_r, sib_s, sib_r, loc_s, rim_s, rim_r, pag_s, pag_r, psib_s, psib_r, str_s,
):
    row, col = lax.axis_index("brow"), lax.axis_index("bcol")
    me = row * BCOL + col
    core = col % 2
    chip = me // 2
    place_own = core * 64 + chip
    sibling = (row, col + 1 - 2 * core)
    dens_refs = (dens0_ref, dens1_ref)

    barrier = pltpu.get_barrier_semaphore()

    def greet(k, carry):
        pl.semaphore_signal(barrier, inc=1, device_id=place((me + k) % DEVICES), device_id_type=MESH)
        return carry

    lax.fori_loop(1, DEVICES, greet, 0)

    owner, slot, node = map_ref[0], map_ref[1], map_ref[2]
    mine = owner == me
    own_owner = map_ref[0, pl.ds(me, 1), :]
    own_slot = map_ref[1, pl.ds(me, 1), :]
    own = jnp.concatenate([own_owner, own_slot, jnp.zeros((6, PANELS), jnp.int32)], axis=0).astype(F32)
    own = jnp.concatenate([own, jnp.zeros((8, 256 - PANELS), F32)], axis=1).T.astype(jnp.int32)[:PANELS]
    for s in range(3):
        here = jnp.where(mine & (slot == s), node + 1, 0)
        at = jnp.sum(here, axis=1, keepdims=True) - 1
        lane = lax.broadcasted_iota(jnp.int32, (DEVICES, NODES), 1)
        tab[s * DEVICES:(s + 1) * DEVICES, :] = jnp.where(lane == at, 1.0, 0.0).astype(BF16)

    def traces_of(ref):
        field16 = ref[...].astype(BF16)
        return [dot_t(tab[s * DEVICES:(s + 1) * DEVICES, :], field16) for s in range(3)]

    def loads_of(pot):
        pot16 = pot.astype(BF16)
        out = []
        for s in range(3):
            pick = (lax.broadcasted_iota(jnp.int32, (DEVICES, PANELS), 0) == own_owner) & (own_slot == s)
            out.append(dot_t(jnp.where(pick, 1.0, 0.0).astype(BF16), pot16))
        return out

    def slab(ref, k):
        return ref.at[pl.ds(pl.multiple_of(k * SLAB, SLAB), SLAB), :]

    def exchange(n, pieces):
        for r in range(0, len(pieces), 2):
            pair = (pieces + pieces[-1:])[r:r + 2]
            send[n][pl.ds(r // 2, DEVICES, stride=SLAB), :] = jnp.concatenate(pair, axis=1)
        if n == 0:
            pl.semaphore_wait(barrier, DEVICES - 1)

        def push(k, carry):
            to = (me + k) % DEVICES
            pltpu.make_async_remote_copy(
                src_ref=slab(send[n], to), dst_ref=slab(recv[n], me), send_sem=a2a_s.at[n], recv_sem=a2a_r.at[n],
                device_id=place(to), device_id_type=MESH,
            ).start()
            return carry

        lax.fori_loop(1, DEVICES, push, 0)
        keep = pl.ds(pl.multiple_of(me * SLAB, SLAB), SLAB)
        recv[n][keep, :] = send[n][keep, :]

    def exchanged(n):
        whole = pl.ds(0, (DEVICES - 1) * SLAB)
        return pltpu.make_async_remote_copy(
            src_ref=send[n].at[whole, :], dst_ref=recv[n].at[whole, :], send_sem=a2a_s.at[n], recv_sem=a2a_r.at[n],
            device_id=sibling, device_id_type=MESH,
        )

    def pieces_of(n, first, count):
        out = []
        for k in range(first, first + count):
            got = recv[n][pl.ds(k // 2, DEVICES, stride=SLAB), :]
            out.append(got[:, (k % 2) * COLS:(k % 2) * COLS + COLS].astype(BF16))
        return out

    def chips(src, dst, s_sem, r_sem):
        def push(k, carry):
            to = ((chip + k) % (DEVICES // 2)) * 2 + core
            pltpu.make_async_remote_copy(
                src_ref=src, dst_ref=dst.at[place_own], send_sem=s_sem, recv_sem=r_sem,
                device_id=place(to), device_id_type=MESH,
            ).start()
            return carry

        lax.fori_loop(1, DEVICES // 2, push, 0)

    def chips_wait(dst, s_sem, r_sem):
        group = dst.at[pl.ds(0, DEVICES // 2 - 1)]
        wait = pltpu.make_async_remote_copy(
            src_ref=group, dst_ref=group, send_sem=s_sem, recv_sem=r_sem, device_id=sibling, device_id_type=MESH,
        )
        wait.wait_recv()
        wait.wait_send()

    def swap_of(dst, s_sem, r_sem):
        half = dst.at[pl.ds(core * 64, 64)]
        return pltpu.make_async_remote_copy(
            src_ref=half, dst_ref=half, send_sem=s_sem, recv_sem=r_sem, device_id=sibling, device_id_type=MESH,
        )

    def gather_dens(n, traces):
        dens = jnp.zeros((PANELS, COLS), F32)
        for s in range(3):
            pick = (lax.broadcasted_iota(jnp.int32, (PANELS, DEVICES), 1) == own[:, 0:1]) & (own[:, 1:2] == s)
            dens += dot(jnp.where(pick, 1.0, 0.0).astype(BF16), traces[s])
        dbuf[n] = jnp.concatenate([dens[:HALF], dens[HALF:]], axis=1).astype(BF16)
        pltpu.make_async_copy(dbuf.at[n], dens_refs[n].at[place_own], loc_s.at[n]).start()
        chips(dbuf.at[n], dens_refs[n], ag_s.at[n], ag_r.at[n])

    def forward_dens(n):
        chips_wait(dens_refs[n], ag_s.at[n], ag_r.at[n])
        pltpu.make_async_copy(dbuf.at[n], dens_refs[n].at[place_own], loc_s.at[n]).wait()
        swap_of(dens_refs[n], sib_s.at[n], sib_r.at[n]).start()

    def set_rhs(loads):
        load_t = jnp.concatenate([x.astype(F32) for x in loads], axis=0).T.astype(BF16)
        for h in range(NODES // CHUNK):
            c = slice(h * CHUNK, (h + 1) * CHUNK)
            rhs[:, c] = force_ref[:, c] + dot(load_t, tab[:, c])

    def rim_copy(step, side):
        return pltpu.make_async_remote_copy(
            src_ref=rim_out.at[step, side], dst_ref=rim_in.at[step, 1 - side], send_sem=rim_s.at[step, side],
            recv_sem=rim_r.at[step, 1 - side], device_id=place(me + 2 * side - 1), device_id_type=MESH,
        )

    def rim_send(step, side, values):
        rim_out[step, side] = values

        @pl.when((me > 0) if side == 0 else (me < DEVICES - 1))
        def _():
            rim_copy(step, side).start()

    def rim_wait(step):
        @pl.when(me > 0)
        def _():
            rim_copy(step, 1).wait_recv()
            rim_copy(step, 0).wait_send()

        @pl.when(me == 0)
        def _():
            rim_in[step, 0] = jnp.zeros((COLS, RIM), F32)

        @pl.when(me < DEVICES - 1)
        def _():
            rim_copy(step, 0).wait_recv()
            rim_copy(step, 1).wait_send()

        @pl.when(me == DEVICES - 1)
        def _():
            rim_in[step, 1] = jnp.zeros((COLS, RIM), F32)

    exchange(0, traces_of(field_ref) + loads_of(pot_ref[...]))
    points = pts_ref[...].astype(F32)
    both = jnp.concatenate([points[:, :HALF], points[:, HALF:], jnp.zeros((2, HALF), F32)], axis=0)
    pts_own[...] = jnp.concatenate([both, jnp.zeros((8, 128 - HALF), F32)], axis=1)
    chips(pts_own, pts_in, pag_s, pag_r)
    pts_in[pl.ds(place_own, 1)] = pts_own[...][None]
    for side in range(2):
        rim_send(0, side, field_ref[:, side * (NODES - RIM):side * (NODES - RIM) + RIM])

    idx = jnp.concatenate([idx_ref[...], jnp.full((PAD - idx_ref.shape[0], ELEMS), -1, jnp.int32)], axis=0)
    idx_t = jnp.concatenate([idx.astype(F32), jnp.zeros((PAD, PAD - ELEMS), F32)], axis=1).T.astype(jnp.int32)
    for e in range(ELEMS):
        at = jnp.broadcast_to(idx[:, e:e + 1], (PAD, 128)).astype(jnp.int16)
        ids = jnp.broadcast_to(idx_t[e:e + 1, :], (PAD, PAD)).astype(jnp.int16)
        one, zero = jnp.ones((PAD, PAD), BF16), jnp.zeros((PAD, PAD), BF16)

        def tiles(h, carry):
            start = pl.multiple_of(h * 128, 128)
            lane = (lax.broadcasted_iota(jnp.int32, (PAD, 128), 1) + start).astype(jnp.int16)
            gt[e * PAD:(e + 1) * PAD, pl.ds(start, 128)] = jnp.where(lane == at, one, zero)
            line = (lax.broadcasted_iota(jnp.int32, (128, PAD), 0) + start).astype(jnp.int16)
            gn[pl.ds(start, 128), e * PAD:(e + 1) * PAD] = jnp.where(line == ids, one, zero)
            return carry

        lax.fori_loop(0, NODES // 128, tiles, 0, unroll=4)
    npe = mat_ref.shape[0]
    mat = jnp.concatenate([mat_ref[...], jnp.zeros((PAD - npe, npe), F32)], axis=0)
    mat = jnp.concatenate([mat, jnp.zeros((PAD, PAD - npe), F32)], axis=1)
    mat = jnp.concatenate(split(mat), axis=1)
    rmass[...] = 1.0 / mass_ref[...]
    out_ref[...] = field_ref[...]
    hi, lo = split(field_ref[...])
    v2[0:COLS, :] = hi
    v2[COLS:, :] = lo
    points = jnp.concatenate([points, jnp.zeros((5, PANELS), F32)], axis=0)
    points = jnp.concatenate([points, jnp.zeros((8, 256 - PANELS), F32)], axis=1).T[:PANELS]
    for k in range(3):
        tgt[k] = jnp.broadcast_to(points[:, k:k + 1], (PANELS, 128))

    exchanged(0).wait_recv()
    gather_dens(0, pieces_of(0, 0, 3))
    set_rhs(pieces_of(0, 3, 3))

    def sweep_gather():
        def gather(i, carry):
            c = pl.ds(pl.multiple_of(i * CHUNK, CHUNK), CHUNK)
            got = dot(v2[...], gn[:, c]).astype(BF16)
            per = CHUNK // PAD
            for k in range(per):
                r = dot(got[:, k * PAD:(k + 1) * PAD], mat)
                y = (r[:COLS, :PAD] + (r[:COLS, PAD:] + r[COLS:, :PAD])) * coef_ref[i * per + k]
                a, b = split(y)
                e = pl.ds(pl.multiple_of(i * CHUNK + k * PAD, PAD), PAD)
                yy[0:COLS, e] = a
                yy[COLS:, e] = b
            return carry

        lax.fori_loop(0, ELEMS * PAD // CHUNK, gather, 0)

    def sweep_update(step):
        last = NODES // CHUNK - 1
        for h in [0, last] + list(range(1, last)):
            c = slice(h * CHUNK, (h + 1) * CHUNK)
            s = dot(yy[...], gt[:, c])
            s = s[:COLS] + s[COLS:]
            if h == 0:
                s = jnp.concatenate([s[:, :RIM] - PENALTY * rim_in[step, 0], s[:, RIM:]], axis=1)
            if h == last:
                s = jnp.concatenate([s[:, :CHUNK - RIM], s[:, CHUNK - RIM:] - PENALTY * rim_in[step, 1]], axis=1)
            now = out_ref[:, c]
            new = now + WEIGHTS[step % SWEEPS] * ((rhs[:, c] - s) * rmass[:, c] - now)
            out_ref[:, c] = new
            if step < STEPS - 1:
                hi, lo = split(new)
                v2[0:COLS, c] = hi
                v2[COLS:, c] = lo
                if h == 0:
                    rim_send(step + 1, 0, new[:, :RIM])
                if h == last:
                    rim_send(step + 1, 1, new[:, CHUNK - RIM:])

    def build(start, stop):
        def unit(u, carry):
            tile, r = u // (PANELS // STEP), u % (PANELS // STEP)
            g, t = tile // GROUP, tile % GROUP
            first = pl.multiple_of(r * STEP, STEP)
            for lane in range(TILE // 128):
                src = pl.ds(pl.multiple_of(tile * TILE + lane * 128, 128), 128)
                dst = pl.ds(pl.multiple_of(t * TILE + lane * 128, 128), 128)
                for half in range(2):
                    d = [
                        pts_all[half * 3 + k:half * 3 + k + 1, src] - tgt[k, pl.ds(first, STEP), :] for k in range(3)
                    ]
                    re, im = kernel_tile(d)
                    kmat[g, pl.ds(half * 2 * PANELS + first, STEP), dst] = re
                    kmat[g, pl.ds(half * 2 * PANELS + PANELS + first, STEP), dst] = im
            return carry

        lax.fori_loop(start, stop, unit, 0, unroll=2)

    for step in range(SWEEPS):
        sweep_gather()
        rim_wait(step)
        sweep_update(step)
        if step == 0:
            chips_wait(pts_in, pag_s, pag_r)
            swap_of(pts_in, psib_s, psib_r).start()

    exchange(1, traces_of(out_ref))
    swap_of(pts_in, psib_s, psib_r).wait()
    for g in range(DEVICES // 4):
        four = jnp.concatenate([pts_in[g * 4 + k][:, :HALF] for k in range(4)], axis=1)
        pts_all[:, g * 384:(g + 1) * 384] = four
    build(0, UNITS // 4)
    exchanged(1).wait_recv()
    gather_dens(1, pieces_of(1, 0, 3))
    forward_dens(0)
    build(UNITS // 4, UNITS - UNITS // 6)
    forward_dens(1)
    build(UNITS - UNITS // 6, UNITS)
    for n in range(2):
        swap_of(dens_refs[n], sib_s.at[n], sib_r.at[n]).wait()

    def fetch(g, n):
        blocks = pl.ds(g * BLOCKS, BLOCKS)
        return pltpu.make_async_copy(dens_refs[n].at[blocks], stream.at[g % 2, n], str_s.at[g % 2, n])

    for n in range(2):
        fetch(0, n).start()
    acc[...] = jnp.zeros_like(acc)

    def product(g, carry):
        @pl.when(g < GROUPS - 1)
        def _():
            for n in range(2):
                fetch(g + 1, n).start()

        for n in range(2):
            fetch(g, n).wait()
        got = stream[g % 2]
        both = jnp.concatenate([got[n].reshape(BLOCKS * HALF, 128) for n in range(2)], axis=1)
        acc[...] += dot(kmat[g], both)
        return carry

    lax.fori_loop(0, GROUPS, product, 0)
    exchanged(1).wait_send()
    exchange(2, loads_of(potential_of(acc, 0)))
    res_ref[...] = potential_of(acc, 1)
    for step in range(SWEEPS, STEPS):
        sweep_gather()
        if step == SWEEPS:
            exchanged(2).wait_recv()
            set_rhs(pieces_of(2, 0, 3))
        rim_wait(step)
        sweep_update(step)
    exchanged(0).wait_send()
    exchanged(2).wait_send()


def per_device(
    panel_points, panel_map, element_nodes, element_coef, element_matrix, node_mass, forcing, field, potential
):
    maps = panel_map.reshape(3, DEVICES, PANELS)
    dma = pltpu.SemaphoreType.DMA
    dens = jax.ShapeDtypeStruct((DEVICES, HALF, 128), BF16)
    slabs = (DEVICES * SLAB, 128)

    def run(*refs):
        refs = list(refs)
        at = 13 + 7
        s0, s1, r0, r1, r2 = refs[at:at + 5]
        refs[at:at + 5] = [(s0, s1, s1), (r0, r1, r2)]
        body(*refs)

    out = pl.pallas_call(
        run,
        out_shape=(
            jax.ShapeDtypeStruct((COLS, NODES), F32), jax.ShapeDtypeStruct((COLS, PANELS), F32), dens, dens,
        ),
        in_specs=[VMEM] * 8 + [pl.BlockSpec(memory_space=pltpu.SMEM)],
        out_specs=(VMEM, VMEM, ANY, ANY),
        scratch_shapes=[
            pltpu.VMEM((NODES, ELEMS * PAD), BF16),
            pltpu.VMEM((ELEMS * PAD, NODES), BF16),
            pltpu.VMEM((GROUPS, ROWS, TILE * GROUP), BF16),
            pltpu.VMEM((2 * COLS, NODES), BF16),
            pltpu.VMEM((2 * COLS, ELEMS * PAD), BF16),
            pltpu.VMEM((COLS, NODES), F32),
            pltpu.VMEM((1, NODES), F32),
            pltpu.VMEM(slabs, F32), pltpu.VMEM(slabs, F32),
            pltpu.VMEM(slabs, F32), pltpu.VMEM(slabs, F32), pltpu.VMEM(slabs, F32),
            pltpu.VMEM((2, HALF, 128), BF16),
            pltpu.VMEM((STEPS, 2, COLS, RIM), F32),
            pltpu.VMEM((STEPS, 2, COLS, RIM), F32),
            pltpu.VMEM((3 * DEVICES, NODES), BF16),
            pltpu.VMEM((8, 128), F32),
            pltpu.VMEM((DEVICES, 8, 128), F32),
            pltpu.VMEM((8, COUNT // 2), F32),
            pltpu.VMEM((3, PANELS, 128), F32),
            pltpu.VMEM((2, 2, BLOCKS, HALF, 128), BF16),
            pltpu.VMEM((ROWS, 256), F32),
            dma((3,)), dma((3,)), dma((2,)), dma((2,)), dma((2,)), dma((2,)), dma((2,)),
            dma((STEPS, 2)), dma((STEPS, 2)), dma, dma, dma, dma, dma((2, 2)),
        ],
        compiler_params=pltpu.CompilerParams(
            collective_id=1, has_side_effects=True, vmem_limit_bytes=67043328
        ),
        name="mega",
    )(maps, element_nodes, element_matrix, node_mass[None, :], forcing, field, potential, panel_points, element_coef)
    return out[0], out[1]


def solution(mesh):
    both = ("brow", "bcol")
    placed = (P(None, both), P(), P(None, both), P(both), P(), P(both), P(None, both), P(None, both), P(None, both))
    return jax.shard_map(
        per_device,
        mesh=mesh,
        in_specs=placed,
        out_specs=(P(None, both), P(None, both)),
        check_vma=False,
    )
```

```python
import functools
import math

import jax
import jax.numpy as jnp
from jax import lax
from jax.experimental import pallas as pl
from jax.experimental.pallas import tpu as pltpu
from jax.sharding import PartitionSpec as P

F32 = jnp.float32
BF16 = jnp.bfloat16
MESH = pl.DeviceIdType.MESH
VMEM = pl.BlockSpec(memory_space=pltpu.VMEM)
ANY = pl.BlockSpec(memory_space=pl.ANY)

RIM = 128
SWEEPS = 3
ITERS = 2
WAVE = 20.0
PENALTY = 0.5
COLS = 64
NODES = 2048
ELEMS = 32
PAD = 128
PANELS = 192
HALF = PANELS // 2
DEVICES = 128
COUNT = PANELS * DEVICES
BCOL = 16
CHUNK = 512
STEPS = SWEEPS * ITERS
TILE = 256
GROUP = 3
GROUPS = COUNT // 2 // (TILE * GROUP)
BLOCKS = TILE * GROUP // HALF
PARTS = 8
SPAN = DEVICES // PARTS
ROWS = 4 * PANELS
STEP = 16
CHUNK_G = 1024
CHUNK_S = 2048
IN_GATHER = 8
IN_SCATTER = 32
UNITS = GROUPS * GROUP * (PANELS // STEP)

WEIGHTS = [
    1.0 / (1.25 + 0.75 * math.cos(math.pi * (2 * m + 1) / (2.0 * SWEEPS))) for m in range(SWEEPS)
]
SOFT2 = (0.5 * float(COUNT) ** (-1.0 / 3.0)) ** 2
NORM = 1.0 / math.sqrt(float(COUNT))
TURN = WAVE / (2.0 * math.pi)
SIN_C = (4.442882919124344, -7.308245686509072, 3.606354218432951, -0.8461116503739222, 0.10982451642504502)
COS_C = (1.4142134962552282, -6.978850948563825, 5.739460376907423, -1.8835579059881276, 0.3106880275291379)


def split(x):
    hi = x.astype(BF16)
    return hi, (x - hi.astype(F32)).astype(BF16)


def dot(a, b):
    return jnp.dot(a, b, preferred_element_type=F32)


def dot_t(a, b):
    return lax.dot_general(a, b, (((1,), (1,)), ((), ())), preferred_element_type=F32)


def dot_l(a, b):
    return lax.dot_general(a, b, (((0,), (0,)), ((), ())), preferred_element_type=F32)


def place(rank):
    return (rank // BCOL, rank % BCOL)


def kernel_tile(d):
    sq = d[0] * d[0] + d[1] * d[1] + (d[2] * d[2] + SOFT2)
    inv = lax.rsqrt(sq)
    turns = (sq * inv) * TURN
    f = turns - jnp.round(turns)
    z = f * f
    sn, cs = SIN_C[4], COS_C[4]
    for k in (3, 2, 1, 0):
        sn = sn * z + SIN_C[k]
        cs = cs * z + COS_C[k]
    sn = sn * f
    scale = inv * NORM
    part = sn * scale
    return (scale - part * sn).astype(BF16), (part * cs).astype(BF16)


def potential_of(acc, n):
    at = n * 128
    real = acc[0:PANELS, at:at + COLS] + acc[2 * PANELS:3 * PANELS, at + COLS:at + 128]
    imag = acc[PANELS:2 * PANELS, at:at + COLS] + acc[3 * PANELS:, at + COLS:at + 128]
    half = COLS // 2
    return (real + jnp.concatenate([-imag[:, half:], imag[:, :half]], axis=1)).T


def body(
    map_ref, idx_ref, mat_ref, mass_ref, force_ref, field_ref, pot_ref, pts_ref, coef_ref,
    out_ref, res_ref, dens0_ref, dens1_ref,
    gn, gt, kmat, v2, yy, rhs, rmass, send, recv, dbuf, rim_out, rim_in, tab, pts_own, pts_in, pts_all, tgt, stream, acc, ids, held,
    a2a_s, a2a_r, ag_s, ag_r, sib_s, sib_r, loc_s, rim_s, rim_r, pag_s, pag_r, psib_s, psib_r, str_s,
):
    row, col = lax.axis_index("brow"), lax.axis_index("bcol")
    me = row * BCOL + col
    core = col % 2
    chip = me // 2
    at_x, at_y, at_z = (row // 4) * 2 + (col // 2) % 2, row % 4, col // 4
    along = (at_x + core * (at_z - at_x), at_y + core * (at_x - at_y), at_z + core * (at_y - at_z))
    place_own = core * 64 + along[2] * 16 + along[1] * 4 + along[0]
    sibling = (row, col + 1 - 2 * core)
    dens_refs = (dens0_ref, dens1_ref)

    barrier = pltpu.get_barrier_semaphore()

    def greet(k, carry):
        pl.semaphore_signal(barrier, inc=1, device_id=place((me + k) % DEVICES), device_id_type=MESH)
        return carry

    lax.fori_loop(1, DEVICES, greet, 0)

    owner, slot, node = map_ref[0], map_ref[1], map_ref[2]
    mine = owner == me
    own_owner = map_ref[0, pl.ds(me, 1), :]
    own_slot = map_ref[1, pl.ds(me, 1), :]
    own = jnp.concatenate([own_owner, own_slot, jnp.zeros((6, PANELS), jnp.int32)], axis=0).astype(F32)
    own = jnp.concatenate([own, jnp.zeros((8, 256 - PANELS), F32)], axis=1).T.astype(jnp.int32)[:PANELS]
    for s in range(3):
        here = jnp.where(mine & (slot == s), node + 1, 0)
        at = jnp.sum(here, axis=1, keepdims=True) - 1
        lane = lax.broadcasted_iota(jnp.int32, (DEVICES, NODES), 1)
        tab[s * DEVICES:(s + 1) * DEVICES, :] = jnp.where(lane == at, 1.0, 0.0).astype(BF16)

    def traces_of(ref):
        field16 = ref[...].astype(BF16)
        return [dot_t(tab[s * DEVICES:(s + 1) * DEVICES, :], field16) for s in range(3)]

    def loads_of(pot):
        pot16 = pot.astype(BF16)
        out = []
        for s in range(3):
            pick = (lax.broadcasted_iota(jnp.int32, (DEVICES, PANELS), 0) == own_owner) & (own_slot == s)
            out.append(dot_t(jnp.where(pick, 1.0, 0.0).astype(BF16), pot16))
        return out

    def exchange(n, pieces):
        for r in range(0, len(pieces), 2):
            pair = (pieces + pieces[-1:])[r:r + 2]
            send[n][:, r // 2, :] = jnp.concatenate(pair, axis=1)
        if n == 0:
            pl.semaphore_wait(barrier, DEVICES - 1)

        def push(k, carry):
            to = (me + k) % DEVICES
            pltpu.make_async_remote_copy(
                src_ref=send[n].at[to], dst_ref=recv[n].at[me], send_sem=a2a_s.at[n], recv_sem=a2a_r.at[n],
                device_id=place(to), device_id_type=MESH,
            ).start()
            return carry

        lax.fori_loop(1, DEVICES, push, 0)
        recv[n][pl.ds(me, 1)] = send[n][pl.ds(me, 1)]

    def exchanged(n):
        whole = pl.ds(0, DEVICES - 1)
        return pltpu.make_async_remote_copy(
            src_ref=send[n].at[whole], dst_ref=recv[n].at[whole], send_sem=a2a_s.at[n], recv_sem=a2a_r.at[n],
            device_id=sibling, device_id_type=MESH,
        )

    def pieces_of(n, first, count):
        out = []
        for k in range(first, first + count):
            got = recv[n][:, k // 2, :]
            out.append(got[:, (k % 2) * COLS:(k % 2) * COLS + COLS].astype(BF16))
        return out

    def chips(src, dst, s_sem, r_sem):
        def push(k, carry):
            to = ((chip + k) % (DEVICES // 2)) * 2 + core
            pltpu.make_async_remote_copy(
                src_ref=src, dst_ref=dst.at[place_own], send_sem=s_sem, recv_sem=r_sem,
                device_id=place(to), device_id_type=MESH,
            ).start()
            return carry

        lax.fori_loop(1, DEVICES // 2, push, 0)

    def chips_wait(dst, s_sem, r_sem):
        group = dst.at[pl.ds(0, DEVICES // 2 - 1)]
        wait = pltpu.make_async_remote_copy(
            src_ref=group, dst_ref=group, send_sem=s_sem, recv_sem=r_sem, device_id=sibling, device_id_type=MESH,
        )
        wait.wait_recv()
        wait.wait_send()

    def swap_of(dst, s_sem, r_sem):
        half = dst.at[pl.ds(core * 64, 64)]
        return pltpu.make_async_remote_copy(
            src_ref=half, dst_ref=half, send_sem=s_sem, recv_sem=r_sem, device_id=sibling, device_id_type=MESH,
        )

    def gather_dens(n, traces):
        dens = jnp.zeros((PANELS, COLS), F32)
        for s in range(3):
            pick = (lax.broadcasted_iota(jnp.int32, (PANELS, DEVICES), 1) == own[:, 0:1]) & (own[:, 1:2] == s)
            dens += dot(jnp.where(pick, 1.0, 0.0).astype(BF16), traces[s])
        dbuf[n] = jnp.concatenate([dens[:HALF], dens[HALF:]], axis=1).astype(BF16)
        pltpu.make_async_copy(dbuf.at[n], dens_refs[n].at[place_own], loc_s.at[n]).start()
        spread(n, 0)

    def spread(n, phase):
        count = 4 ** phase
        base = core * 64 + along[2] * 16 + (along[1] * 4 if phase < 2 else 0) + (along[0] if phase < 1 else 0)
        group = dens_refs[n].at[pl.ds(base, count)]

        def push(k, carry):
            to = [(a + k) % 4 if axis == phase else a for axis, a in enumerate(along)]
            x, y, z = to[0] + core * (to[1] - to[0]), to[1] + core * (to[2] - to[1]), to[2] + core * (to[0] - to[2])
            pltpu.make_async_remote_copy(
                src_ref=dbuf.at[pl.ds(n, 1)] if phase == 0 else group, dst_ref=group,
                send_sem=ag_s.at[n, phase], recv_sem=ag_r.at[n, phase],
                device_id=((x // 2) * 4 + y, z * 4 + (x % 2) * 2 + core), device_id_type=MESH,
            ).start()
            return carry

        lax.fori_loop(1, 4, push, 0)

    def spread_wait(n, phase):
        group = dens_refs[n].at[pl.ds(0, 3 * 4 ** phase)]
        wait = pltpu.make_async_remote_copy(
            src_ref=group, dst_ref=group, send_sem=ag_s.at[n, phase], recv_sem=ag_r.at[n, phase],
            device_id=sibling, device_id_type=MESH,
        )
        wait.wait_recv()
        wait.wait_send()
        if phase == 0:
            pltpu.make_async_copy(dbuf.at[n], dens_refs[n].at[place_own], loc_s.at[n]).wait()

    def spread_on(n, phase):
        spread_wait(n, phase - 1)
        if phase < 3:
            spread(n, phase)
        else:
            swap_of(dens_refs[n], sib_s.at[n], sib_r.at[n]).start()

    def set_rhs(loads):
        load_t = jnp.concatenate([x.astype(F32) for x in loads], axis=0).T.astype(BF16)
        for h in range(NODES // CHUNK):
            c = slice(h * CHUNK, (h + 1) * CHUNK)
            rhs[:, c] = force_ref[:, c] + dot(load_t, tab[:, c])

    def rim_copy(step, side):
        return pltpu.make_async_remote_copy(
            src_ref=rim_out.at[step, side], dst_ref=rim_in.at[step, 1 - side], send_sem=rim_s.at[step, side],
            recv_sem=rim_r.at[step, 1 - side], device_id=place(me + 2 * side - 1), device_id_type=MESH,
        )

    def rim_send(step, side, values):
        rim_out[step, side] = values

        @pl.when((me > 0) if side == 0 else (me < DEVICES - 1))
        def _():
            rim_copy(step, side).start()

    def rim_wait(step):
        @pl.when(me > 0)
        def _():
            rim_copy(step, 1).wait_recv()
            rim_copy(step, 0).wait_send()

        @pl.when(me == 0)
        def _():
            rim_in[step, 0] = jnp.zeros((COLS, RIM), F32)

        @pl.when(me < DEVICES - 1)
        def _():
            rim_copy(step, 0).wait_recv()
            rim_copy(step, 1).wait_send()

        @pl.when(me == DEVICES - 1)
        def _():
            rim_in[step, 1] = jnp.zeros((COLS, RIM), F32)

    exchange(0, traces_of(field_ref) + loads_of(pot_ref[...]))
    points = pts_ref[...].astype(F32)
    both = jnp.concatenate([points[:, :HALF], points[:, HALF:], jnp.zeros((2, HALF), F32)], axis=0)
    pts_own[...] = jnp.concatenate([both, jnp.zeros((8, 128 - HALF), F32)], axis=1)
    chips(pts_own, pts_in, pag_s, pag_r)
    pts_in[pl.ds(place_own, 1)] = pts_own[...][None]
    for side in range(2):
        rim_send(0, side, field_ref[:, side * (NODES - RIM):side * (NODES - RIM) + RIM])

    idx = jnp.concatenate([idx_ref[...], jnp.full((PAD - idx_ref.shape[0], ELEMS), -1, jnp.int32)], axis=0)
    idx_t = jnp.concatenate([idx.astype(F32), jnp.zeros((PAD, PAD - ELEMS), F32)], axis=1).T.astype(jnp.int32)
    ids[...] = idx_t[:ELEMS]

    def tables(e, carry):
        row_id = jnp.broadcast_to(ids[pl.ds(e, 1), :], (PAD, PAD))
        low = jnp.where((row_id & 127) == lax.broadcasted_iota(jnp.int32, (PAD, PAD), 0), 1.0, 0.0)
        high = (row_id >> 7).astype(F32)
        low_t, high_t = low.T.astype(BF16), high.T.astype(BF16)
        low, high = low.astype(BF16), high.astype(BF16)
        zero = jnp.zeros((PAD, PAD), BF16)
        at = pl.ds(pl.multiple_of(e * PAD, PAD), PAD)
        for h in range(NODES // 128):
            gt[at, h * 128:(h + 1) * 128] = jnp.where(high_t == jnp.asarray(h, BF16), low_t, zero)
            gn[h * 128:(h + 1) * 128, at] = jnp.where(high == jnp.asarray(h, BF16), low, zero)
        return carry

    lax.fori_loop(0, ELEMS, tables, 0, unroll=2)
    npe = mat_ref.shape[0]
    mat = jnp.concatenate([mat_ref[...], jnp.zeros((PAD - npe, npe), F32)], axis=0)
    mat = jnp.concatenate([mat, jnp.zeros((PAD, PAD - npe), F32)], axis=1)
    mat_hi, mat_lo = split(mat)
    mat = jnp.concatenate(
        [jnp.concatenate([mat_hi, mat_lo], axis=1), jnp.concatenate([mat_hi, jnp.zeros_like(mat_lo)], axis=1)], axis=0
    )
    rmass[...] = 1.0 / mass_ref[...]
    out_ref[...] = field_ref[...]
    hi, lo = split(field_ref[...])
    v2[0:COLS, :] = hi
    v2[COLS:, :] = lo
    points = jnp.concatenate([points, jnp.zeros((5, PANELS), F32)], axis=0)
    points = jnp.concatenate([points, jnp.zeros((8, 256 - PANELS), F32)], axis=1).T[:PANELS]
    for k in range(3):
        tgt[k] = jnp.broadcast_to(points[:, k:k + 1], (PANELS, 128))

    exchanged(0).wait_recv()
    gather_dens(0, pieces_of(0, 0, 3))
    set_rhs(pieces_of(0, 3, 3))

    def unit(u):
        tile, r = u // (PANELS // STEP), u % (PANELS // STEP)
        g, t = tile // GROUP, tile % GROUP
        first = pl.multiple_of(r * STEP, STEP)
        for lane in range(TILE // 128):
            src = pl.ds(pl.multiple_of(tile * TILE + lane * 128, 128), 128)
            dst = pl.ds(pl.multiple_of(t * TILE + lane * 128, 128), 128)
            for half in range(2):
                d = [pts_all[half * 3 + k:half * 3 + k + 1, src] - tgt[k, pl.ds(first, STEP), :] for k in range(3)]
                re, im = kernel_tile(d)
                kmat[g, pl.ds(half * 2 * PANELS + first, STEP), dst] = re
                kmat[g, pl.ds(half * 2 * PANELS + PANELS + first, STEP), dst] = im

    def build(start, stop):
        def step(u, carry):
            unit(u)
            return carry

        lax.fori_loop(start, stop, step, 0, unroll=2)

    def sweep_gather(start=None):
        def gather(i, carry):
            c = pl.ds(pl.multiple_of(i * CHUNK_G, CHUNK_G), CHUNK_G)
            if start is not None:
                for k in range(IN_GATHER):
                    unit(start + i * IN_GATHER + k)
            got = dot(v2[...], gn[:, c]).astype(BF16)
            per = CHUNK_G // PAD
            got = jnp.concatenate(
                [
                    jnp.concatenate([got[:COLS, k * PAD:(k + 1) * PAD], got[COLS:, k * PAD:(k + 1) * PAD]], axis=1)
                    for k in range(per)
                ], axis=0,
            )
            r = dot(got, mat)
            for k in range(per):
                at = slice(k * COLS, (k + 1) * COLS)
                y = (r[at, :PAD] + r[at, PAD:]) * coef_ref[i * per + k]
                a, b = split(y)
                e = pl.ds(pl.multiple_of(i * CHUNK_G + k * PAD, PAD), PAD)
                yy[0:COLS, e] = a
                yy[COLS:, e] = b
            return carry

        lax.fori_loop(0, ELEMS * PAD // CHUNK_G, gather, 0)

    def sweep_scatter(start=None):
        def scatter(h, carry):
            c = pl.ds(pl.multiple_of(h * CHUNK_S, CHUNK_S), CHUNK_S)
            if start is not None:
                for k in range(IN_SCATTER):
                    unit(start + h * IN_SCATTER + k)
            s = dot(yy[...], gt[:, c])
            held[:, c] = s[:COLS] + s[COLS:]
            return carry

        lax.fori_loop(0, NODES // CHUNK_S, scatter, 0)

    def sweep_update(step):
        last = NODES // CHUNK - 1
        for h in [0, last] + list(range(1, last)):
            c = slice(h * CHUNK, (h + 1) * CHUNK)
            s = held[:, c]
            if h == 0:
                s = jnp.concatenate([s[:, :RIM] - PENALTY * rim_in[step, 0], s[:, RIM:]], axis=1)
            if h == last:
                s = jnp.concatenate([s[:, :CHUNK - RIM], s[:, CHUNK - RIM:] - PENALTY * rim_in[step, 1]], axis=1)
            now = out_ref[:, c]
            new = now + WEIGHTS[step % SWEEPS] * ((rhs[:, c] - s) * rmass[:, c] - now)
            out_ref[:, c] = new
            if step < STEPS - 1:
                hi, lo = split(new)
                v2[0:COLS, c] = hi
                v2[COLS:, c] = lo
                if h == 0:
                    rim_send(step + 1, 0, new[:, :RIM])
                if h == last:
                    rim_send(step + 1, 1, new[:, CHUNK - RIM:])

    per_gather, per_scatter = IN_GATHER * (ELEMS * PAD // CHUNK_G), IN_SCATTER * (NODES // CHUNK_S)
    chips_wait(pts_in, pag_s, pag_r)
    swap_of(pts_in, psib_s, psib_r).start()
    sweep_gather()
    swap_of(pts_in, psib_s, psib_r).wait()
    for g in range(DEVICES // 4):
        four = jnp.concatenate([pts_in[g * 4 + k][:, :HALF] for k in range(4)], axis=1)
        pts_all[:, g * 384:(g + 1) * 384] = four
    sweep_scatter(0)
    done = per_scatter
    rim_wait(0)
    sweep_update(0)
    spread_on(0, 1)
    for step in range(1, SWEEPS):
        sweep_gather(done)
        done += per_gather
        rim_wait(step)
        if step == SWEEPS - 1:
            spread_on(0, 2)
        sweep_scatter(done)
        done += per_scatter
        sweep_update(step)
    exchange(1, traces_of(out_ref))
    sweep_gather(done)
    done += per_gather
    spread_on(0, 3)
    exchanged(1).wait_recv()
    gather_dens(1, pieces_of(1, 0, 3))
    sweep_scatter(done)
    done += per_scatter
    spread_on(1, 1)
    part = (UNITS - done) // 8
    build(done, done + 2 * part)
    spread_on(1, 2)
    build(done + 2 * part, done + 6 * part)
    spread_on(1, 3)
    build(done + 6 * part, UNITS)
    for n in range(2):
        swap_of(dens_refs[n], sib_s.at[n], sib_r.at[n]).wait()

    def fetch(p, n):
        return pltpu.make_async_copy(
            dens_refs[n].at[pl.ds(p * SPAN, SPAN)], stream.at[p % 2, n], str_s.at[p % 2, n]
        )

    for n in range(2):
        fetch(0, n).start()
    for p in range(PARTS):
        for n in range(2):
            if p < PARTS - 1:
                fetch(p + 1, n).start()
            fetch(p, n).wait()

        def rows(r, carry):
            at = pl.ds(pl.multiple_of(r * TILE, TILE), TILE)
            total = jnp.zeros((TILE, 256), F32) if p == 0 else acc[at, :]
            for g in range(GROUPS // PARTS):
                both = [stream[p % 2, n, g * BLOCKS:(g + 1) * BLOCKS].reshape(BLOCKS * HALF, 128) for n in range(2)]
                total += dot(kmat[p * (GROUPS // PARTS) + g, at, :], jnp.concatenate(both, axis=1))
            acc[at, :] = total
            return carry

        lax.fori_loop(0, ROWS // TILE, rows, 0)

    exchange(2, loads_of(potential_of(acc, 0)))
    res_ref[...] = potential_of(acc, 1)
    rim_wait(SWEEPS)
    exchanged(2).wait_recv()
    set_rhs(pieces_of(2, 0, 3))
    sweep_update(SWEEPS)
    for step in range(SWEEPS + 1, STEPS):
        sweep_gather()
        rim_wait(step)
        sweep_scatter()
        sweep_update(step)
    for n in range(3):
        exchanged(n).wait_send()


def per_device(
    panel_points, panel_map, element_nodes, element_coef, element_matrix, node_mass, forcing, field, potential
):
    maps = panel_map.reshape(3, DEVICES, PANELS)
    dma = pltpu.SemaphoreType.DMA
    dens = jax.ShapeDtypeStruct((DEVICES, HALF, 128), BF16)

    def run(*refs):
        refs = list(refs)
        at = 13 + 7
        refs[at:at + 6] = [tuple(refs[at:at + 3]), tuple(refs[at + 3:at + 6])]
        body(*refs)

    out = pl.pallas_call(
        run,
        out_shape=(
            jax.ShapeDtypeStruct((COLS, NODES), F32), jax.ShapeDtypeStruct((COLS, PANELS), F32), dens, dens,
        ),
        in_specs=[VMEM] * 8 + [pl.BlockSpec(memory_space=pltpu.SMEM)],
        out_specs=(VMEM, VMEM, ANY, ANY),
        scratch_shapes=[
            pltpu.VMEM((NODES, ELEMS * PAD), BF16),
            pltpu.VMEM((ELEMS * PAD, NODES), BF16),
            pltpu.VMEM((GROUPS, ROWS, TILE * GROUP), BF16),
            pltpu.VMEM((2 * COLS, NODES), BF16),
            pltpu.VMEM((2 * COLS, ELEMS * PAD), BF16),
            pltpu.VMEM((COLS, NODES), F32),
            pltpu.VMEM((1, NODES), F32),
            pltpu.VMEM((DEVICES, 4, 128), F32), pltpu.VMEM((DEVICES, 2, 128), F32), pltpu.VMEM((DEVICES, 2, 128), F32),
            pltpu.VMEM((DEVICES, 4, 128), F32), pltpu.VMEM((DEVICES, 2, 128), F32), pltpu.VMEM((DEVICES, 2, 128), F32),
            pltpu.VMEM((2, HALF, 128), BF16),
            pltpu.VMEM((STEPS, 2, COLS, RIM), F32),
            pltpu.VMEM((STEPS, 2, COLS, RIM), F32),
            pltpu.VMEM((3 * DEVICES, NODES), BF16),
            pltpu.VMEM((8, 128), F32),
            pltpu.VMEM((DEVICES, 8, 128), F32),
            pltpu.VMEM((8, COUNT // 2), F32),
            pltpu.VMEM((3, PANELS, 128), F32),
            pltpu.VMEM((2, 2, SPAN, HALF, 128), BF16),
            pltpu.VMEM((ROWS, 256), F32),
            pltpu.VMEM((ELEMS, PAD), jnp.int32),
            pltpu.VMEM((COLS, NODES), F32),
            dma((3,)), dma((3,)), dma((2, 3)), dma((2, 3)), dma((2,)), dma((2,)), dma((2,)),
            dma((STEPS, 2)), dma((STEPS, 2)), dma, dma, dma, dma, dma((2, 2)),
        ],
        compiler_params=pltpu.CompilerParams(
            collective_id=1, has_side_effects=True, vmem_limit_bytes=67043328
        ),
        name="mega",
    )(maps, element_nodes, element_matrix, node_mass[None, :], forcing, field, potential, panel_points, element_coef)
    return out[0], out[1]


def solution(mesh):
    both = ("brow", "bcol")
    placed = (P(None, both), P(), P(None, both), P(both), P(), P(both), P(None, both), P(None, both), P(None, both))
    return jax.shard_map(
        per_device,
        mesh=mesh,
        in_specs=placed,
        out_specs=(P(None, both), P(None, both)),
        check_vma=False,
    )
```

```python
import functools
import math

import jax
import jax.numpy as jnp
from jax import lax
from jax.experimental import pallas as pl
from jax.experimental.pallas import tpu as pltpu
from jax.sharding import PartitionSpec as P

F32 = jnp.float32
BF16 = jnp.bfloat16
MESH = pl.DeviceIdType.MESH
VMEM = pl.BlockSpec(memory_space=pltpu.VMEM)
ANY = pl.BlockSpec(memory_space=pl.ANY)

RIM = 128
SWEEPS = 3
ITERS = 2
WAVE = 20.0
PENALTY = 0.5
COLS = 64
NODES = 2048
ELEMS = 32
PAD = 128
PANELS = 192
HALF = PANELS // 2
DEVICES = 128
COUNT = PANELS * DEVICES
BCOL = 16
CHUNK = 512
STEPS = SWEEPS * ITERS
TILE = 256
GROUP = 3
GROUPS = COUNT // 2 // (TILE * GROUP)
BLOCKS = TILE * GROUP // HALF
PARTS = 8
SPAN = DEVICES // PARTS
ROWS = 4 * PANELS
STEP = 16
CHUNK_G = 1024
CHUNK_S = 1024
UNITS = GROUPS * GROUP * (PANELS // STEP)

WEIGHTS = [
    1.0 / (1.25 + 0.75 * math.cos(math.pi * (2 * m + 1) / (2.0 * SWEEPS))) for m in range(SWEEPS)
]
SOFT2 = (0.5 * float(COUNT) ** (-1.0 / 3.0)) ** 2
NORM = 1.0 / math.sqrt(float(COUNT))
TURN = WAVE / (2.0 * math.pi)
SIN_C = (4.442882919124344, -7.308245686509072, 3.606354218432951, -0.8461116503739222, 0.10982451642504502)
COS_C = (1.4142134962552282, -6.978850948563825, 5.739460376907423, -1.8835579059881276, 0.3106880275291379)


def split(x):
    hi = x.astype(BF16)
    return hi, (x - hi.astype(F32)).astype(BF16)


def dot(a, b):
    return jnp.dot(a, b, preferred_element_type=F32)


def dot_t(a, b):
    return lax.dot_general(a, b, (((1,), (1,)), ((), ())), preferred_element_type=F32)


def dot_l(a, b):
    return lax.dot_general(a, b, (((0,), (0,)), ((), ())), preferred_element_type=F32)


def place(rank):
    return (rank // BCOL, rank % BCOL)


def kernel_tile(d):
    sq = d[0] * d[0] + d[1] * d[1] + (d[2] * d[2] + SOFT2)
    inv = lax.rsqrt(sq)
    turns = (sq * inv) * TURN
    f = turns - jnp.round(turns)
    z = f * f
    sn, cs = SIN_C[4], COS_C[4]
    for k in (3, 2, 1, 0):
        sn = sn * z + SIN_C[k]
        cs = cs * z + COS_C[k]
    sn = sn * f
    scale = inv * NORM
    part = sn * scale
    return (scale - part * sn).astype(BF16), (part * cs).astype(BF16)


def potential_of(acc, n):
    at = n * 128
    real = acc[0:PANELS, at:at + COLS] + acc[2 * PANELS:3 * PANELS, at + COLS:at + 128]
    imag = acc[PANELS:2 * PANELS, at:at + COLS] + acc[3 * PANELS:, at + COLS:at + 128]
    half = COLS // 2
    return (real + jnp.concatenate([-imag[:, half:], imag[:, :half]], axis=1)).T


def body(
    map_ref, idx_ref, mat_ref, mass_ref, force_ref, field_ref, pot_ref, pts_ref, coef_ref,
    out_ref, res_ref, dens0_ref, dens1_ref,
    gn, gt, kmat, v2, yy, rhs, rmass, send, recv, dbuf, rim_out, rim_in, tab, pts_own, pts_in, pts_all, tgt, stream, acc, ids, held,
    a2a_s, a2a_r, ag_s, ag_r, sib_s, sib_r, loc_s, rim_s, rim_r, pag_s, pag_r, psib_s, psib_r, str_s,
):
    row, col = lax.axis_index("brow"), lax.axis_index("bcol")
    me = row * BCOL + col
    core = col % 2
    chip = me // 2
    at_x, at_y, at_z = (row // 4) * 2 + (col // 2) % 2, row % 4, col // 4
    along = (at_x + core * (at_z - at_x), at_y + core * (at_x - at_y), at_z + core * (at_y - at_z))
    place_own = core * 64 + along[2] * 16 + along[1] * 4 + along[0]
    sibling = (row, col + 1 - 2 * core)
    dens_refs = (dens0_ref, dens1_ref)

    barrier = pltpu.get_barrier_semaphore()

    def greet(k, carry):
        pl.semaphore_signal(barrier, inc=1, device_id=place((me + k) % DEVICES), device_id_type=MESH)
        return carry

    lax.fori_loop(1, DEVICES, greet, 0)

    owner, slot, node = map_ref[0], map_ref[1], map_ref[2]
    mine = owner == me
    own_owner = map_ref[0, pl.ds(me, 1), :]
    own_slot = map_ref[1, pl.ds(me, 1), :]
    own = jnp.concatenate([own_owner, own_slot, jnp.zeros((6, PANELS), jnp.int32)], axis=0).astype(F32)
    own = jnp.concatenate([own, jnp.zeros((8, 256 - PANELS), F32)], axis=1).T.astype(jnp.int32)[:PANELS]
    for s in range(3):
        here = jnp.where(mine & (slot == s), node + 1, 0)
        at = jnp.sum(here, axis=1, keepdims=True) - 1
        lane = lax.broadcasted_iota(jnp.int32, (DEVICES, NODES), 1)
        tab[s * DEVICES:(s + 1) * DEVICES, :] = jnp.where(lane == at, 1.0, 0.0).astype(BF16)

    def traces_of(ref):
        field16 = ref[...].astype(BF16)
        return [dot_t(tab[s * DEVICES:(s + 1) * DEVICES, :], field16) for s in range(3)]

    def loads_of(pot):
        pot16 = pot.astype(BF16)
        out = []
        for s in range(3):
            pick = (lax.broadcasted_iota(jnp.int32, (DEVICES, PANELS), 0) == own_owner) & (own_slot == s)
            out.append(dot_t(jnp.where(pick, 1.0, 0.0).astype(BF16), pot16))
        return out

    def exchange(n, pieces):
        for r in range(0, len(pieces), 2):
            pair = (pieces + pieces[-1:])[r:r + 2]
            send[n][:, r // 2, :] = jnp.concatenate(pair, axis=1)
        if n == 0:
            pl.semaphore_wait(barrier, DEVICES - 1)

        def push(k, carry):
            to = (me + k) % DEVICES
            pltpu.make_async_remote_copy(
                src_ref=send[n].at[to], dst_ref=recv[n].at[me], send_sem=a2a_s.at[n], recv_sem=a2a_r.at[n],
                device_id=place(to), device_id_type=MESH,
            ).start()
            return carry

        lax.fori_loop(1, DEVICES, push, 0)
        recv[n][pl.ds(me, 1)] = send[n][pl.ds(me, 1)]

    def exchanged(n):
        whole = pl.ds(0, DEVICES - 1)
        return pltpu.make_async_remote_copy(
            src_ref=send[n].at[whole], dst_ref=recv[n].at[whole], send_sem=a2a_s.at[n], recv_sem=a2a_r.at[n],
            device_id=sibling, device_id_type=MESH,
        )

    def pieces_of(n, first, count):
        out = []
        for k in range(first, first + count):
            got = recv[n][:, k // 2, :]
            out.append(got[:, (k % 2) * COLS:(k % 2) * COLS + COLS].astype(BF16))
        return out

    def chips(src, dst, s_sem, r_sem):
        def push(k, carry):
            to = ((chip + k) % (DEVICES // 2)) * 2 + core
            pltpu.make_async_remote_copy(
                src_ref=src, dst_ref=dst.at[place_own], send_sem=s_sem, recv_sem=r_sem,
                device_id=place(to), device_id_type=MESH,
            ).start()
            return carry

        lax.fori_loop(1, DEVICES // 2, push, 0)

    def chips_wait(dst, s_sem, r_sem):
        group = dst.at[pl.ds(0, DEVICES // 2 - 1)]
        wait = pltpu.make_async_remote_copy(
            src_ref=group, dst_ref=group, send_sem=s_sem, recv_sem=r_sem, device_id=sibling, device_id_type=MESH,
        )
        wait.wait_recv()
        wait.wait_send()

    def swap_of(dst, s_sem, r_sem):
        half = dst.at[pl.ds(core * 64, 64)]
        return pltpu.make_async_remote_copy(
            src_ref=half, dst_ref=half, send_sem=s_sem, recv_sem=r_sem, device_id=sibling, device_id_type=MESH,
        )

    def gather_dens(n, traces):
        dens = jnp.zeros((PANELS, COLS), F32)
        for s in range(3):
            pick = (lax.broadcasted_iota(jnp.int32, (PANELS, DEVICES), 1) == own[:, 0:1]) & (own[:, 1:2] == s)
            dens += dot(jnp.where(pick, 1.0, 0.0).astype(BF16), traces[s])
        dbuf[n] = jnp.concatenate([dens[:HALF], dens[HALF:]], axis=1).astype(BF16)
        pltpu.make_async_copy(dbuf.at[n], dens_refs[n].at[place_own], loc_s.at[n]).start()
        spread(n, 0)

    def spread(n, phase):
        count = 4 ** phase
        base = core * 64 + along[2] * 16 + (along[1] * 4 if phase < 2 else 0) + (along[0] if phase < 1 else 0)
        group = dens_refs[n].at[pl.ds(base, count)]

        def push(k, carry):
            to = [(a + k) % 4 if axis == phase else a for axis, a in enumerate(along)]
            x, y, z = to[0] + core * (to[1] - to[0]), to[1] + core * (to[2] - to[1]), to[2] + core * (to[0] - to[2])
            pltpu.make_async_remote_copy(
                src_ref=dbuf.at[pl.ds(n, 1)] if phase == 0 else group, dst_ref=group,
                send_sem=ag_s.at[n, phase], recv_sem=ag_r.at[n, phase],
                device_id=((x // 2) * 4 + y, z * 4 + (x % 2) * 2 + core), device_id_type=MESH,
            ).start()
            return carry

        lax.fori_loop(1, 4, push, 0)

    def spread_wait(n, phase):
        group = dens_refs[n].at[pl.ds(0, 3 * 4 ** phase)]
        wait = pltpu.make_async_remote_copy(
            src_ref=group, dst_ref=group, send_sem=ag_s.at[n, phase], recv_sem=ag_r.at[n, phase],
            device_id=sibling, device_id_type=MESH,
        )
        wait.wait_recv()
        wait.wait_send()
        if phase == 0:
            pltpu.make_async_copy(dbuf.at[n], dens_refs[n].at[place_own], loc_s.at[n]).wait()

    def spread_on(n, phase):
        spread_wait(n, phase - 1)
        if phase < 3:
            spread(n, phase)
        else:
            swap_of(dens_refs[n], sib_s.at[n], sib_r.at[n]).start()

    def set_rhs(loads):
        load_t = jnp.concatenate([x.astype(F32) for x in loads], axis=0).T.astype(BF16)
        for h in range(NODES // CHUNK):
            c = slice(h * CHUNK, (h + 1) * CHUNK)
            rhs[:, c] = force_ref[:, c] + dot(load_t, tab[:, c])

    def rim_copy(step, side):
        return pltpu.make_async_remote_copy(
            src_ref=rim_out.at[step, side], dst_ref=rim_in.at[step, 1 - side], send_sem=rim_s.at[step, side],
            recv_sem=rim_r.at[step, 1 - side], device_id=place(me + 2 * side - 1), device_id_type=MESH,
        )

    def rim_send(step, side, values):
        rim_out[step, side] = values

        @pl.when((me > 0) if side == 0 else (me < DEVICES - 1))
        def _():
            rim_copy(step, side).start()

    def rim_wait(step):
        @pl.when(me > 0)
        def _():
            rim_copy(step, 1).wait_recv()
            rim_copy(step, 0).wait_send()

        @pl.when(me == 0)
        def _():
            rim_in[step, 0] = jnp.zeros((COLS, RIM), F32)

        @pl.when(me < DEVICES - 1)
        def _():
            rim_copy(step, 0).wait_recv()
            rim_copy(step, 1).wait_send()

        @pl.when(me == DEVICES - 1)
        def _():
            rim_in[step, 1] = jnp.zeros((COLS, RIM), F32)

    exchange(0, traces_of(field_ref) + loads_of(pot_ref[...]))
    points = pts_ref[...].astype(F32)
    both = jnp.concatenate([points[:, :HALF], points[:, HALF:], jnp.zeros((2, HALF), F32)], axis=0)
    pts_own[...] = jnp.concatenate([both, jnp.zeros((8, 128 - HALF), F32)], axis=1)
    chips(pts_own, pts_in, pag_s, pag_r)
    pts_in[pl.ds(place_own, 1)] = pts_own[...][None]
    for side in range(2):
        rim_send(0, side, field_ref[:, side * (NODES - RIM):side * (NODES - RIM) + RIM])

    idx = jnp.concatenate([idx_ref[...], jnp.full((PAD - idx_ref.shape[0], ELEMS), -1, jnp.int32)], axis=0)
    idx_t = jnp.concatenate([idx.astype(F32), jnp.zeros((PAD, PAD - ELEMS), F32)], axis=1).T.astype(jnp.int32)
    ids[...] = idx_t[:ELEMS]

    def tables(e, carry):
        row_id = jnp.broadcast_to(ids[pl.ds(e, 1), :], (PAD, PAD))
        low = jnp.where((row_id & 127) == lax.broadcasted_iota(jnp.int32, (PAD, PAD), 0), 1.0, 0.0)
        high = (row_id >> 7).astype(F32)
        low_t, high_t = low.T.astype(BF16), high.T.astype(BF16)
        low, high = low.astype(BF16), high.astype(BF16)
        zero = jnp.zeros((PAD, PAD), BF16)
        at = pl.ds(pl.multiple_of(e * PAD, PAD), PAD)
        for h in range(NODES // 128):
            gt[at, h * 128:(h + 1) * 128] = jnp.where(high_t == jnp.asarray(h, BF16), low_t, zero)
            gn[h * 128:(h + 1) * 128, at] = jnp.where(high == jnp.asarray(h, BF16), low, zero)
        return carry

    lax.fori_loop(0, ELEMS, tables, 0, unroll=2)
    npe = mat_ref.shape[0]
    mat = jnp.concatenate([mat_ref[...], jnp.zeros((PAD - npe, npe), F32)], axis=0)
    mat = jnp.concatenate([mat, jnp.zeros((PAD, PAD - npe), F32)], axis=1)
    mat_hi, mat_lo = split(mat)
    mat = jnp.concatenate(
        [jnp.concatenate([mat_hi, mat_lo], axis=1), jnp.concatenate([mat_hi, jnp.zeros_like(mat_lo)], axis=1)], axis=0
    )
    rmass[...] = 1.0 / mass_ref[...]
    out_ref[...] = field_ref[...]
    hi, lo = split(field_ref[...])
    v2[0:COLS, :] = hi
    v2[COLS:, :] = lo
    points = jnp.concatenate([points, jnp.zeros((5, PANELS), F32)], axis=0)
    points = jnp.concatenate([points, jnp.zeros((8, 256 - PANELS), F32)], axis=1).T[:PANELS]
    for k in range(3):
        tgt[k] = jnp.broadcast_to(points[:, k:k + 1], (PANELS, 128))

    exchanged(0).wait_recv()
    gather_dens(0, pieces_of(0, 0, 3))
    set_rhs(pieces_of(0, 3, 3))

    def unit(u):
        tile, r = u // (PANELS // STEP), u % (PANELS // STEP)
        g, t = tile // GROUP, tile % GROUP
        first = pl.multiple_of(r * STEP, STEP)
        for lane in range(TILE // 128):
            src = pl.ds(pl.multiple_of(tile * TILE + lane * 128, 128), 128)
            dst = pl.ds(pl.multiple_of(t * TILE + lane * 128, 128), 128)
            for half in range(2):
                d = [pts_all[half * 3 + k:half * 3 + k + 1, src] - tgt[k, pl.ds(first, STEP), :] for k in range(3)]
                re, im = kernel_tile(d)
                kmat[g, pl.ds(half * 2 * PANELS + first, STEP), dst] = re
                kmat[g, pl.ds(half * 2 * PANELS + PANELS + first, STEP), dst] = im

    def build(start, stop):
        def step(u, carry):
            unit(u)
            return carry

        lax.fori_loop(start, stop, step, 0, unroll=2)

    def sweep_gather():
        def gather(i, carry):
            c = pl.ds(pl.multiple_of(i * CHUNK_G, CHUNK_G), CHUNK_G)
            got = dot(v2[...], gn[:, c]).astype(BF16)
            per = CHUNK_G // PAD
            got = jnp.concatenate(
                [
                    jnp.concatenate([got[:COLS, k * PAD:(k + 1) * PAD], got[COLS:, k * PAD:(k + 1) * PAD]], axis=1)
                    for k in range(per)
                ], axis=0,
            )
            r = dot(got, mat)
            for k in range(per):
                at = slice(k * COLS, (k + 1) * COLS)
                y = (r[at, :PAD] + r[at, PAD:]) * coef_ref[i * per + k]
                a, b = split(y)
                e = pl.ds(pl.multiple_of(i * CHUNK_G + k * PAD, PAD), PAD)
                yy[0:COLS, e] = a
                yy[COLS:, e] = b
            return carry

        lax.fori_loop(0, ELEMS * PAD // CHUNK_G, gather, 0)

    def sweep_scatter():
        def scatter(h, carry):
            c = pl.ds(pl.multiple_of(h * CHUNK_S, CHUNK_S), CHUNK_S)
            s = dot(yy[...], gt[:, c])
            held[:, c] = s[:COLS] + s[COLS:]
            return carry

        lax.fori_loop(0, NODES // CHUNK_S, scatter, 0)

    def sweep_update(step):
        last = NODES // CHUNK - 1
        for h in [0, last] + list(range(1, last)):
            c = slice(h * CHUNK, (h + 1) * CHUNK)
            s = held[:, c]
            if h == 0:
                s = jnp.concatenate([s[:, :RIM] - PENALTY * rim_in[step, 0], s[:, RIM:]], axis=1)
            if h == last:
                s = jnp.concatenate([s[:, :CHUNK - RIM], s[:, CHUNK - RIM:] - PENALTY * rim_in[step, 1]], axis=1)
            now = out_ref[:, c]
            new = now + WEIGHTS[step % SWEEPS] * ((rhs[:, c] - s) * rmass[:, c] - now)
            out_ref[:, c] = new
            if step < STEPS - 1:
                hi, lo = split(new)
                v2[0:COLS, c] = hi
                v2[COLS:, c] = lo
                if h == 0:
                    rim_send(step + 1, 0, new[:, :RIM])
                if h == last:
                    rim_send(step + 1, 1, new[:, CHUNK - RIM:])

    for step in range(SWEEPS):
        sweep_gather()
        if step == 0:
            chips_wait(pts_in, pag_s, pag_r)
            swap_of(pts_in, psib_s, psib_r).start()
        sweep_scatter()
        rim_wait(step)
        sweep_update(step)
        if step < SWEEPS - 1:
            spread_on(0, step + 1)
    exchange(1, traces_of(out_ref))
    swap_of(pts_in, psib_s, psib_r).wait()
    for g in range(DEVICES // 4):
        four = jnp.concatenate([pts_in[g * 4 + k][:, :HALF] for k in range(4)], axis=1)
        pts_all[:, g * 384:(g + 1) * 384] = four
    part = UNITS // 8
    build(0, 2 * part)
    spread_on(0, 3)
    exchanged(1).wait_recv()
    gather_dens(1, pieces_of(1, 0, 3))
    build(2 * part, 3 * part)
    spread_on(1, 1)
    build(3 * part, 4 * part)
    spread_on(1, 2)
    build(4 * part, 7 * part)
    spread_on(1, 3)
    build(7 * part, UNITS)
    for n in range(2):
        swap_of(dens_refs[n], sib_s.at[n], sib_r.at[n]).wait()

    def fetch(p, n):
        return pltpu.make_async_copy(
            dens_refs[n].at[pl.ds(p * SPAN, SPAN)], stream.at[p % 2, n], str_s.at[p % 2, n]
        )

    for n in range(2):
        fetch(0, n).start()
    for p in range(PARTS):
        for n in range(2):
            if p < PARTS - 1:
                fetch(p + 1, n).start()
            fetch(p, n).wait()

        def rows(r, carry):
            at = pl.ds(pl.multiple_of(r * TILE, TILE), TILE)
            total = jnp.zeros((TILE, 256), F32) if p == 0 else acc[at, :]
            for g in range(GROUPS // PARTS):
                both = [stream[p % 2, n, g * BLOCKS:(g + 1) * BLOCKS].reshape(BLOCKS * HALF, 128) for n in range(2)]
                total += dot(kmat[p * (GROUPS // PARTS) + g, at, :], jnp.concatenate(both, axis=1))
            acc[at, :] = total
            return carry

        lax.fori_loop(0, ROWS // TILE, rows, 0)

    exchange(2, loads_of(potential_of(acc, 0)))
    res_ref[...] = potential_of(acc, 1)
    for step in range(SWEEPS, STEPS):
        sweep_gather()
        sweep_scatter()
        if step == SWEEPS:
            exchanged(2).wait_recv()
            set_rhs(pieces_of(2, 0, 3))
        rim_wait(step)
        sweep_update(step)
    for n in range(3):
        exchanged(n).wait_send()


def per_device(
    panel_points, panel_map, element_nodes, element_coef, element_matrix, node_mass, forcing, field, potential
):
    maps = panel_map.reshape(3, DEVICES, PANELS)
    dma = pltpu.SemaphoreType.DMA
    dens = jax.ShapeDtypeStruct((DEVICES, HALF, 128), BF16)

    def run(*refs):
        refs = list(refs)
        at = 13 + 7
        refs[at:at + 6] = [tuple(refs[at:at + 3]), tuple(refs[at + 3:at + 6])]
        body(*refs)

    out = pl.pallas_call(
        run,
        out_shape=(
            jax.ShapeDtypeStruct((COLS, NODES), F32), jax.ShapeDtypeStruct((COLS, PANELS), F32), dens, dens,
        ),
        in_specs=[VMEM] * 8 + [pl.BlockSpec(memory_space=pltpu.SMEM)],
        out_specs=(VMEM, VMEM, ANY, ANY),
        scratch_shapes=[
            pltpu.VMEM((NODES, ELEMS * PAD), BF16),
            pltpu.VMEM((ELEMS * PAD, NODES), BF16),
            pltpu.VMEM((GROUPS, ROWS, TILE * GROUP), BF16),
            pltpu.VMEM((2 * COLS, NODES), BF16),
            pltpu.VMEM((2 * COLS, ELEMS * PAD), BF16),
            pltpu.VMEM((COLS, NODES), F32),
            pltpu.VMEM((1, NODES), F32),
            pltpu.VMEM((DEVICES, 4, 128), F32), pltpu.VMEM((DEVICES, 2, 128), F32), pltpu.VMEM((DEVICES, 2, 128), F32),
            pltpu.VMEM((DEVICES, 4, 128), F32), pltpu.VMEM((DEVICES, 2, 128), F32), pltpu.VMEM((DEVICES, 2, 128), F32),
            pltpu.VMEM((2, HALF, 128), BF16),
            pltpu.VMEM((STEPS, 2, COLS, RIM), F32),
            pltpu.VMEM((STEPS, 2, COLS, RIM), F32),
            pltpu.VMEM((3 * DEVICES, NODES), BF16),
            pltpu.VMEM((8, 128), F32),
            pltpu.VMEM((DEVICES, 8, 128), F32),
            pltpu.VMEM((8, COUNT // 2), F32),
            pltpu.VMEM((3, PANELS, 128), F32),
            pltpu.VMEM((2, 2, SPAN, HALF, 128), BF16),
            pltpu.VMEM((ROWS, 256), F32),
            pltpu.VMEM((ELEMS, PAD), jnp.int32),
            pltpu.VMEM((COLS, NODES), F32),
            dma((3,)), dma((3,)), dma((2, 3)), dma((2, 3)), dma((2,)), dma((2,)), dma((2,)),
            dma((STEPS, 2)), dma((STEPS, 2)), dma, dma, dma, dma, dma((2, 2)),
        ],
        compiler_params=pltpu.CompilerParams(
            collective_id=1, has_side_effects=True, vmem_limit_bytes=67043328
        ),
        name="mega",
    )(maps, element_nodes, element_matrix, node_mass[None, :], forcing, field, potential, panel_points, element_coef)
    return out[0], out[1]


def solution(mesh):
    both = ("brow", "bcol")
    placed = (P(None, both), P(), P(None, both), P(both), P(), P(both), P(None, both), P(None, both), P(None, both))
    return jax.shard_map(
        per_device,
        mesh=mesh,
        in_specs=placed,
        out_specs=(P(None, both), P(None, both)),
        check_vma=False,
    )
```

```python
import functools
import math

import jax
import jax.numpy as jnp
from jax import lax
from jax.experimental import pallas as pl
from jax.experimental.pallas import tpu as pltpu
from jax.sharding import PartitionSpec as P

F32 = jnp.float32
BF16 = jnp.bfloat16
MESH = pl.DeviceIdType.MESH
VMEM = pl.BlockSpec(memory_space=pltpu.VMEM)
ANY = pl.BlockSpec(memory_space=pl.ANY)

RIM = 128
SWEEPS = 3
ITERS = 2
WAVE = 20.0
PENALTY = 0.5
COLS = 64
NODES = 2048
ELEMS = 32
PAD = 128
PANELS = 192
HALF = PANELS // 2
DEVICES = 128
COUNT = PANELS * DEVICES
BCOL = 16
CHUNK = 512
STEPS = SWEEPS * ITERS
TILE = 256
GROUP = 3
GROUPS = COUNT // 2 // (TILE * GROUP)
BLOCKS = TILE * GROUP // HALF
PARTS = 8
SPAN = DEVICES // PARTS
ROWS = 4 * PANELS
STEP = 16
CHUNK_G = 1024
CHUNK_S = 1024
UNITS = GROUPS * GROUP * (PANELS // STEP)

WEIGHTS = [
    1.0 / (1.25 + 0.75 * math.cos(math.pi * (2 * m + 1) / (2.0 * SWEEPS))) for m in range(SWEEPS)
]
SOFT2 = (0.5 * float(COUNT) ** (-1.0 / 3.0)) ** 2
NORM = 1.0 / math.sqrt(float(COUNT))
TURN = WAVE / (2.0 * math.pi)
SIN_C = (4.442882919124344, -7.308245686509072, 3.606354218432951, -0.8461116503739222, 0.10982451642504502)
COS_C = (1.4142134962552282, -6.978850948563825, 5.739460376907423, -1.8835579059881276, 0.3106880275291379)


def split(x):
    hi = x.astype(BF16)
    return hi, (x - hi.astype(F32)).astype(BF16)


def dot(a, b):
    return jnp.dot(a, b, preferred_element_type=F32)


def dot_t(a, b):
    return lax.dot_general(a, b, (((1,), (1,)), ((), ())), preferred_element_type=F32)


def dot_l(a, b):
    return lax.dot_general(a, b, (((0,), (0,)), ((), ())), preferred_element_type=F32)


def place(rank):
    return (rank // BCOL, rank % BCOL)


def kernel_tile(d):
    sq = d[0] * d[0] + d[1] * d[1] + (d[2] * d[2] + SOFT2)
    inv = lax.rsqrt(sq)
    turns = (sq * inv) * TURN
    f = turns - jnp.round(turns)
    z = f * f
    sn, cs = SIN_C[4], COS_C[4]
    for k in (3, 2, 1, 0):
        sn = sn * z + SIN_C[k]
        cs = cs * z + COS_C[k]
    sn = sn * f
    scale = inv * NORM
    part = sn * scale
    return (scale - part * sn).astype(BF16), (part * cs).astype(BF16)


def potential_of(acc, n):
    at = n * 128
    real = acc[0:PANELS, at:at + COLS] + acc[2 * PANELS:3 * PANELS, at + COLS:at + 128]
    imag = acc[PANELS:2 * PANELS, at:at + COLS] + acc[3 * PANELS:, at + COLS:at + 128]
    half = COLS // 2
    return (real + jnp.concatenate([-imag[:, half:], imag[:, :half]], axis=1)).T


def body(
    map_ref, idx_ref, mat_ref, mass_ref, force_ref, field_ref, pot_ref, pts_ref, coef_ref,
    out_ref, res_ref, dens0_ref, dens1_ref,
    gn, gt, kmat, v2, yy, rhs, rmass, send, recv, dbuf, rim_out, rim_in, tab, pts_own, pts_in, pts_all, tgt, stream, acc, ids, held,
    a2a_s, a2a_r, ag_s, ag_r, sib_s, sib_r, loc_s, rim_s, rim_r, pag_s, pag_r, psib_s, psib_r, str_s,
):
    row, col = lax.axis_index("brow"), lax.axis_index("bcol")
    me = row * BCOL + col
    core = col % 2
    chip = me // 2
    at_x, at_y, at_z = (row // 4) * 2 + (col // 2) % 2, row % 4, col // 4
    along = (at_x + core * (at_z - at_x), at_y + core * (at_x - at_y), at_z + core * (at_y - at_z))
    place_own = core * 64 + along[2] * 16 + along[1] * 4 + along[0]
    sibling = (row, col + 1 - 2 * core)
    dens_refs = (dens0_ref, dens1_ref)

    barrier = pltpu.get_barrier_semaphore()

    def greet(k, carry):
        pl.semaphore_signal(barrier, inc=1, device_id=place((me + k) % DEVICES), device_id_type=MESH)
        return carry

    lax.fori_loop(1, DEVICES, greet, 0)

    owner, slot, node = map_ref[0], map_ref[1], map_ref[2]
    mine = owner == me
    own_owner = map_ref[0, pl.ds(me, 1), :]
    own_slot = map_ref[1, pl.ds(me, 1), :]
    own = jnp.concatenate([own_owner, own_slot, jnp.zeros((6, PANELS), jnp.int32)], axis=0).astype(F32)
    own = jnp.concatenate([own, jnp.zeros((8, 256 - PANELS), F32)], axis=1).T.astype(jnp.int32)[:PANELS]
    for s in range(3):
        here = jnp.where(mine & (slot == s), node + 1, 0)
        at = jnp.sum(here, axis=1, keepdims=True) - 1
        lane = lax.broadcasted_iota(jnp.int32, (DEVICES, NODES), 1)
        tab[s * DEVICES:(s + 1) * DEVICES, :] = jnp.where(lane == at, 1.0, 0.0).astype(BF16)

    def traces_of(ref):
        field16 = ref[...].astype(BF16)
        return [dot_t(tab[s * DEVICES:(s + 1) * DEVICES, :], field16) for s in range(3)]

    def loads_of(pot):
        pot16 = pot.astype(BF16)
        out = []
        for s in range(3):
            pick = (lax.broadcasted_iota(jnp.int32, (DEVICES, PANELS), 0) == own_owner) & (own_slot == s)
            out.append(dot_t(jnp.where(pick, 1.0, 0.0).astype(BF16), pot16))
        return out

    def exchange(n, pieces):
        for r in range(0, len(pieces), 2):
            pair = (pieces + pieces[-1:])[r:r + 2]
            send[n][:, r // 2, :] = jnp.concatenate(pair, axis=1)
        if n == 0:
            pl.semaphore_wait(barrier, DEVICES - 1)

        def push(k, carry):
            to = (me + k) % DEVICES
            pltpu.make_async_remote_copy(
                src_ref=send[n].at[to], dst_ref=recv[n].at[me], send_sem=a2a_s.at[n], recv_sem=a2a_r.at[n],
                device_id=place(to), device_id_type=MESH,
            ).start()
            return carry

        lax.fori_loop(1, DEVICES, push, 0)
        recv[n][pl.ds(me, 1)] = send[n][pl.ds(me, 1)]

    def exchanged(n):
        whole = pl.ds(0, DEVICES - 1)
        return pltpu.make_async_remote_copy(
            src_ref=send[n].at[whole], dst_ref=recv[n].at[whole], send_sem=a2a_s.at[n], recv_sem=a2a_r.at[n],
            device_id=sibling, device_id_type=MESH,
        )

    def pieces_of(n, first, count):
        out = []
        for k in range(first, first + count):
            got = recv[n][:, k // 2, :]
            out.append(got[:, (k % 2) * COLS:(k % 2) * COLS + COLS].astype(BF16))
        return out

    def chips(src, dst, s_sem, r_sem):
        def push(k, carry):
            to = ((chip + k) % (DEVICES // 2)) * 2 + core
            pltpu.make_async_remote_copy(
                src_ref=src, dst_ref=dst.at[place_own], send_sem=s_sem, recv_sem=r_sem,
                device_id=place(to), device_id_type=MESH,
            ).start()
            return carry

        lax.fori_loop(1, DEVICES // 2, push, 0)

    def chips_wait(dst, s_sem, r_sem):
        group = dst.at[pl.ds(0, DEVICES // 2 - 1)]
        wait = pltpu.make_async_remote_copy(
            src_ref=group, dst_ref=group, send_sem=s_sem, recv_sem=r_sem, device_id=sibling, device_id_type=MESH,
        )
        wait.wait_recv()
        wait.wait_send()

    def swap_of(dst, s_sem, r_sem):
        half = dst.at[pl.ds(core * 64, 64)]
        return pltpu.make_async_remote_copy(
            src_ref=half, dst_ref=half, send_sem=s_sem, recv_sem=r_sem, device_id=sibling, device_id_type=MESH,
        )

    def gather_dens(n, traces):
        dens = jnp.zeros((PANELS, COLS), F32)
        for s in range(3):
            pick = (lax.broadcasted_iota(jnp.int32, (PANELS, DEVICES), 1) == own[:, 0:1]) & (own[:, 1:2] == s)
            dens += dot(jnp.where(pick, 1.0, 0.0).astype(BF16), traces[s])
        dbuf[n] = jnp.concatenate([dens[:HALF], dens[HALF:]], axis=1).astype(BF16)
        pltpu.make_async_copy(dbuf.at[n], dens_refs[n].at[place_own], loc_s.at[n]).start()
        spread(n, 0)

    def spread(n, phase):
        count = 4 ** phase
        base = core * 64 + along[2] * 16 + (along[1] * 4 if phase < 2 else 0) + (along[0] if phase < 1 else 0)
        group = dens_refs[n].at[pl.ds(base, count)]

        def push(k, carry):
            to = [(a + k) % 4 if axis == phase else a for axis, a in enumerate(along)]
            x, y, z = to[0] + core * (to[1] - to[0]), to[1] + core * (to[2] - to[1]), to[2] + core * (to[0] - to[2])
            pltpu.make_async_remote_copy(
                src_ref=dbuf.at[pl.ds(n, 1)] if phase == 0 else group, dst_ref=group,
                send_sem=ag_s.at[n, phase], recv_sem=ag_r.at[n, phase],
                device_id=((x // 2) * 4 + y, z * 4 + (x % 2) * 2 + core), device_id_type=MESH,
            ).start()
            return carry

        lax.fori_loop(1, 4, push, 0)

    def spread_wait(n, phase):
        group = dens_refs[n].at[pl.ds(0, 3 * 4 ** phase)]
        wait = pltpu.make_async_remote_copy(
            src_ref=group, dst_ref=group, send_sem=ag_s.at[n, phase], recv_sem=ag_r.at[n, phase],
            device_id=sibling, device_id_type=MESH,
        )
        wait.wait_recv()
        wait.wait_send()
        if phase == 0:
            pltpu.make_async_copy(dbuf.at[n], dens_refs[n].at[place_own], loc_s.at[n]).wait()

    def spread_on(n, phase):
        spread_wait(n, phase - 1)
        if phase < 3:
            spread(n, phase)
        else:
            swap_of(dens_refs[n], sib_s.at[n], sib_r.at[n]).start()

    def set_rhs(loads):
        load_t = jnp.concatenate([x.astype(F32) for x in loads], axis=0).T.astype(BF16)
        for h in range(NODES // CHUNK):
            c = slice(h * CHUNK, (h + 1) * CHUNK)
            rhs[:, c] = force_ref[:, c] + dot(load_t, tab[:, c])

    def rim_copy(step, side):
        return pltpu.make_async_remote_copy(
            src_ref=rim_out.at[step, side], dst_ref=rim_in.at[step, 1 - side], send_sem=rim_s.at[step, side],
            recv_sem=rim_r.at[step, 1 - side], device_id=place(me + 2 * side - 1), device_id_type=MESH,
        )

    def rim_send(step, side, values):
        rim_out[step, side] = values

        @pl.when((me > 0) if side == 0 else (me < DEVICES - 1))
        def _():
            rim_copy(step, side).start()

    def rim_wait(step):
        @pl.when(me > 0)
        def _():
            rim_copy(step, 1).wait_recv()
            rim_copy(step, 0).wait_send()

        @pl.when(me == 0)
        def _():
            rim_in[step, 0] = jnp.zeros((COLS, RIM), F32)

        @pl.when(me < DEVICES - 1)
        def _():
            rim_copy(step, 0).wait_recv()
            rim_copy(step, 1).wait_send()

        @pl.when(me == DEVICES - 1)
        def _():
            rim_in[step, 1] = jnp.zeros((COLS, RIM), F32)

    exchange(0, traces_of(field_ref) + loads_of(pot_ref[...]))
    points = pts_ref[...].astype(F32)
    both = jnp.concatenate([points[:, :HALF], points[:, HALF:], jnp.zeros((2, HALF), F32)], axis=0)
    pts_own[...] = jnp.concatenate([both, jnp.zeros((8, 128 - HALF), F32)], axis=1)
    chips(pts_own, pts_in, pag_s, pag_r)
    pts_in[pl.ds(place_own, 1)] = pts_own[...][None]
    for side in range(2):
        rim_send(0, side, field_ref[:, side * (NODES - RIM):side * (NODES - RIM) + RIM])

    idx = jnp.concatenate([idx_ref[...], jnp.full((PAD - idx_ref.shape[0], ELEMS), -1, jnp.int32)], axis=0)
    idx_t = jnp.concatenate([idx.astype(F32), jnp.zeros((PAD, PAD - ELEMS), F32)], axis=1).T.astype(jnp.int32)
    ids[...] = idx_t[:ELEMS]

    def tables(e, carry):
        row_id = jnp.broadcast_to(ids[pl.ds(e, 1), :], (PAD, PAD))
        low = jnp.where((row_id & 127) == lax.broadcasted_iota(jnp.int32, (PAD, PAD), 0), 1.0, 0.0)
        high = (row_id >> 7).astype(F32)
        low_t, high_t = low.T.astype(BF16), high.T.astype(BF16)
        low, high = low.astype(BF16), high.astype(BF16)
        zero = jnp.zeros((PAD, PAD), BF16)
        at = pl.ds(pl.multiple_of(e * PAD, PAD), PAD)
        for h in range(NODES // 128):
            gt[at, h * 128:(h + 1) * 128] = jnp.where(high_t == jnp.asarray(h, BF16), low_t, zero)
            gn[h * 128:(h + 1) * 128, at] = jnp.where(high == jnp.asarray(h, BF16), low, zero)
        return carry

    lax.fori_loop(0, ELEMS, tables, 0, unroll=2)
    npe = mat_ref.shape[0]
    mat = jnp.concatenate([mat_ref[...], jnp.zeros((PAD - npe, npe), F32)], axis=0)
    mat = jnp.concatenate([mat, jnp.zeros((PAD, PAD - npe), F32)], axis=1)
    mat_hi, mat_lo = split(mat)
    mat = jnp.concatenate(
        [jnp.concatenate([mat_hi, mat_lo], axis=1), jnp.concatenate([mat_hi, jnp.zeros_like(mat_lo)], axis=1)], axis=0
    )
    rmass[...] = 1.0 / mass_ref[...]
    out_ref[...] = field_ref[...]
    hi, lo = split(field_ref[...])
    v2[0:COLS, :] = hi
    v2[COLS:, :] = lo
    points = jnp.concatenate([points, jnp.zeros((5, PANELS), F32)], axis=0)
    points = jnp.concatenate([points, jnp.zeros((8, 256 - PANELS), F32)], axis=1).T[:PANELS]
    for k in range(3):
        tgt[k] = jnp.broadcast_to(points[:, k:k + 1], (PANELS, 128))

    exchanged(0).wait_recv()
    gather_dens(0, pieces_of(0, 0, 3))
    set_rhs(pieces_of(0, 3, 3))

    def unit(u):
        tile, r = u // (PANELS // STEP), u % (PANELS // STEP)
        g, t = tile // GROUP, tile % GROUP
        first = pl.multiple_of(r * STEP, STEP)
        for lane in range(TILE // 128):
            src = pl.ds(pl.multiple_of(tile * TILE + lane * 128, 128), 128)
            dst = pl.ds(pl.multiple_of(t * TILE + lane * 128, 128), 128)
            for half in range(2):
                d = [pts_all[half * 3 + k:half * 3 + k + 1, src] - tgt[k, pl.ds(first, STEP), :] for k in range(3)]
                re, im = kernel_tile(d)
                kmat[g, pl.ds(half * 2 * PANELS + first, STEP), dst] = re
                kmat[g, pl.ds(half * 2 * PANELS + PANELS + first, STEP), dst] = im

    def build(start, stop):
        def step(u, carry):
            unit(u)
            return carry

        lax.fori_loop(start, stop, step, 0, unroll=4)

    def sweep_gather():
        def gather(i, carry):
            c = pl.ds(pl.multiple_of(i * CHUNK_G, CHUNK_G), CHUNK_G)
            got = dot(v2[...], gn[:, c]).astype(BF16)
            per = CHUNK_G // PAD
            got = jnp.concatenate(
                [
                    jnp.concatenate([got[:COLS, k * PAD:(k + 1) * PAD], got[COLS:, k * PAD:(k + 1) * PAD]], axis=1)
                    for k in range(per)
                ], axis=0,
            )
            r = dot(got, mat)
            for k in range(per):
                at = slice(k * COLS, (k + 1) * COLS)
                y = (r[at, :PAD] + r[at, PAD:]) * coef_ref[i * per + k]
                a, b = split(y)
                e = pl.ds(pl.multiple_of(i * CHUNK_G + k * PAD, PAD), PAD)
                yy[0:COLS, e] = a
                yy[COLS:, e] = b
            return carry

        lax.fori_loop(0, ELEMS * PAD // CHUNK_G, gather, 0)

    def sweep_scatter():
        def scatter(h, carry):
            c = pl.ds(pl.multiple_of(h * CHUNK_S, CHUNK_S), CHUNK_S)
            s = dot(yy[...], gt[:, c])
            held[:, c] = s[:COLS] + s[COLS:]
            return carry

        lax.fori_loop(0, NODES // CHUNK_S, scatter, 0)

    def sweep_update(step):
        last = NODES // CHUNK - 1
        for h in [0, last] + list(range(1, last)):
            c = slice(h * CHUNK, (h + 1) * CHUNK)
            s = held[:, c]
            if h == 0:
                s = jnp.concatenate([s[:, :RIM] - PENALTY * rim_in[step, 0], s[:, RIM:]], axis=1)
            if h == last:
                s = jnp.concatenate([s[:, :CHUNK - RIM], s[:, CHUNK - RIM:] - PENALTY * rim_in[step, 1]], axis=1)
            now = out_ref[:, c]
            new = now + WEIGHTS[step % SWEEPS] * ((rhs[:, c] - s) * rmass[:, c] - now)
            out_ref[:, c] = new
            if step < STEPS - 1:
                hi, lo = split(new)
                v2[0:COLS, c] = hi
                v2[COLS:, c] = lo
                if h == 0:
                    rim_send(step + 1, 0, new[:, :RIM])
                if h == last:
                    rim_send(step + 1, 1, new[:, CHUNK - RIM:])

    for step in range(SWEEPS):
        sweep_gather()
        if step == 0:
            chips_wait(pts_in, pag_s, pag_r)
            swap_of(pts_in, psib_s, psib_r).start()
        sweep_scatter()
        rim_wait(step)
        sweep_update(step)
        if step < SWEEPS - 1:
            spread_on(0, step + 1)
    exchange(1, traces_of(out_ref))
    swap_of(pts_in, psib_s, psib_r).wait()
    for g in range(DEVICES // 4):
        four = jnp.concatenate([pts_in[g * 4 + k][:, :HALF] for k in range(4)], axis=1)
        pts_all[:, g * 384:(g + 1) * 384] = four
    part = UNITS // 8
    build(0, 2 * part)
    spread_on(0, 3)
    exchanged(1).wait_recv()
    gather_dens(1, pieces_of(1, 0, 3))
    build(2 * part, 3 * part)
    spread_on(1, 1)
    build(3 * part, 4 * part)
    spread_on(1, 2)
    build(4 * part, 7 * part)
    spread_on(1, 3)
    build(7 * part, UNITS)
    for n in range(2):
        swap_of(dens_refs[n], sib_s.at[n], sib_r.at[n]).wait()

    def fetch(p, n):
        return pltpu.make_async_copy(
            dens_refs[n].at[pl.ds(p * SPAN, SPAN)], stream.at[p % 2, n], str_s.at[p % 2, n]
        )

    for n in range(2):
        fetch(0, n).start()
    for p in range(PARTS):
        for n in range(2):
            if p < PARTS - 1:
                fetch(p + 1, n).start()
            fetch(p, n).wait()

        def rows(r, carry):
            at = pl.ds(pl.multiple_of(r * TILE, TILE), TILE)
            total = jnp.zeros((TILE, 256), F32) if p == 0 else acc[at, :]
            for g in range(GROUPS // PARTS):
                both = [stream[p % 2, n, g * BLOCKS:(g + 1) * BLOCKS].reshape(BLOCKS * HALF, 128) for n in range(2)]
                total += dot(kmat[p * (GROUPS // PARTS) + g, at, :], jnp.concatenate(both, axis=1))
            acc[at, :] = total
            return carry

        lax.fori_loop(0, ROWS // TILE, rows, 0)

    exchange(2, loads_of(potential_of(acc, 0)))
    res_ref[...] = potential_of(acc, 1)
    for step in range(SWEEPS, STEPS):
        sweep_gather()
        sweep_scatter()
        if step == SWEEPS:
            exchanged(2).wait_recv()
            set_rhs(pieces_of(2, 0, 3))
        rim_wait(step)
        sweep_update(step)
    for n in range(3):
        exchanged(n).wait_send()


def per_device(
    panel_points, panel_map, element_nodes, element_coef, element_matrix, node_mass, forcing, field, potential
):
    maps = panel_map.reshape(3, DEVICES, PANELS)
    dma = pltpu.SemaphoreType.DMA
    dens = jax.ShapeDtypeStruct((DEVICES, HALF, 128), BF16)

    def run(*refs):
        refs = list(refs)
        at = 13 + 7
        refs[at:at + 6] = [tuple(refs[at:at + 3]), tuple(refs[at + 3:at + 6])]
        body(*refs)

    out = pl.pallas_call(
        run,
        out_shape=(
            jax.ShapeDtypeStruct((COLS, NODES), F32), jax.ShapeDtypeStruct((COLS, PANELS), F32), dens, dens,
        ),
        in_specs=[VMEM] * 8 + [pl.BlockSpec(memory_space=pltpu.SMEM)],
        out_specs=(VMEM, VMEM, ANY, ANY),
        scratch_shapes=[
            pltpu.VMEM((NODES, ELEMS * PAD), BF16),
            pltpu.VMEM((ELEMS * PAD, NODES), BF16),
            pltpu.VMEM((GROUPS, ROWS, TILE * GROUP), BF16),
            pltpu.VMEM((2 * COLS, NODES), BF16),
            pltpu.VMEM((2 * COLS, ELEMS * PAD), BF16),
            pltpu.VMEM((COLS, NODES), F32),
            pltpu.VMEM((1, NODES), F32),
            pltpu.VMEM((DEVICES, 4, 128), F32), pltpu.VMEM((DEVICES, 2, 128), F32), pltpu.VMEM((DEVICES, 2, 128), F32),
            pltpu.VMEM((DEVICES, 4, 128), F32), pltpu.VMEM((DEVICES, 2, 128), F32), pltpu.VMEM((DEVICES, 2, 128), F32),
            pltpu.VMEM((2, HALF, 128), BF16),
            pltpu.VMEM((STEPS, 2, COLS, RIM), F32),
            pltpu.VMEM((STEPS, 2, COLS, RIM), F32),
            pltpu.VMEM((3 * DEVICES, NODES), BF16),
            pltpu.VMEM((8, 128), F32),
            pltpu.VMEM((DEVICES, 8, 128), F32),
            pltpu.VMEM((8, COUNT // 2), F32),
            pltpu.VMEM((3, PANELS, 128), F32),
            pltpu.VMEM((2, 2, SPAN, HALF, 128), BF16),
            pltpu.VMEM((ROWS, 256), F32),
            pltpu.VMEM((ELEMS, PAD), jnp.int32),
            pltpu.VMEM((COLS, NODES), F32),
            dma((3,)), dma((3,)), dma((2, 3)), dma((2, 3)), dma((2,)), dma((2,)), dma((2,)),
            dma((STEPS, 2)), dma((STEPS, 2)), dma, dma, dma, dma, dma((2, 2)),
        ],
        compiler_params=pltpu.CompilerParams(
            collective_id=1, has_side_effects=True, vmem_limit_bytes=67043328
        ),
        name="mega",
    )(maps, element_nodes, element_matrix, node_mass[None, :], forcing, field, potential, panel_points, element_coef)
    return out[0], out[1]


def solution(mesh):
    both = ("brow", "bcol")
    placed = (P(None, both), P(), P(None, both), P(both), P(), P(both), P(None, both), P(None, both), P(None, both))
    return jax.shard_map(
        per_device,
        mesh=mesh,
        in_specs=placed,
        out_specs=(P(None, both), P(None, both)),
        check_vma=False,
    )
```
